32 devices in a mesh: gx: 4 (over x, core), gy: 8 (over z, y).
Axes of the slice: x: 2, y: 2, z: 4, core: 2. Of those that a mesh axis runs over, the one named last changes fastest.
Arguments:
- blocks: float32 [8, 8, 9, 128, 128], P('gx', 'gy'), may hold values from -0.0625 to 0.0625
- pair_mask: int32 [8, 8, 9, 8, 8], P('gx', 'gy'), may hold values 0 or 1
- rhs_rows: float32 [8, 8, 9, 128, 128], P('gx', 'gy'), may hold values from -6 to 6
- counts: int32 [8, 8, 8], P('gx', 'gy'), may hold values from 1 to 3, as said below
Outputs:
- solution: float32 [8, 8, 9, 128, 128], P('gx', 'gy')
The draws below stay inside these ranges and needn't reach their ends.
Inputs may be any that keep to these rules, and one draw needn't show every extreme that they name: `counts`: cut the first block index into runs of 2 blocks. Within each second index b, run a and run a + 2 together hold at most 2 blocks that have an atom with a count of 2 or more, and some run holds 2 such blocks; at least one atom takes 3 iterations and at least one takes 1.
All inputs are finite; a program needn't handle non-finite values. No bound on the sum of `pair_mask` on one device may be relied on, other than what follows from the above.
Results may differ from the reference program's by a relative error of at most 0.0003.
Values sent between devices are 32-bit elements; how exact they have to be, the bound alone decides.
A program may use at most 128 MiB of HBM per device.

```python
import jax
import jax.numpy as jnp
from jax import lax

ORB = 16
ATOMS = 8
B = 128
OFFSETS = 9
GRP_X = 2
ITERS = 3
NGX = 8
NGY = 8


def draw_counts(key, part):
    groups = NGX // GRP_X
    half_groups = groups // 2
    pair_count = half_groups * NGY
    key_total = jax.random.fold_in(key, 21)
    key_split = jax.random.fold_in(key, 22)
    key_forced = jax.random.fold_in(key, 23)
    key_scores = jax.random.fold_in(key, 24)
    key_base = jax.random.fold_in(key, 25)
    key_leading = jax.random.fold_in(key, 26)
    key_lead_val = jax.random.fold_in(key, 27)
    totals = jax.random.randint(key_total, (pair_count,), 0, GRP_X + 1, dtype=jnp.int32)
    lower = jax.random.randint(key_split, (pair_count,), 0, totals + 1, dtype=jnp.int32)
    forced = jax.random.randint(key_forced, (), 0, pair_count, dtype=jnp.int32)
    pair_ids = jnp.arange(pair_count, dtype=jnp.int32)
    totals = jnp.where(pair_ids == forced, GRP_X, totals)
    lower = jnp.where(pair_ids == forced, GRP_X, lower)
    upper = totals - lower
    loads = jnp.concatenate([lower.reshape(half_groups, NGY), upper.reshape(half_groups, NGY)], axis=0)
    local_ids = jnp.arange(GRP_X, dtype=jnp.int32)
    scores = jax.random.randint(key_scores, (groups, NGY, GRP_X), 0, 1 << 20, dtype=jnp.int32) * GRP_X + local_ids
    ranks = jnp.argsort(jnp.argsort(scores, axis=-1), axis=-1).astype(jnp.int32)
    slow = ranks < loads[..., None]
    base_counts = jax.random.randint(key_base, (groups, NGY, GRP_X, ATOMS), 1, 4, dtype=jnp.int32)
    leading = jax.random.randint(key_leading, (groups, NGY, GRP_X), 0, ATOMS, dtype=jnp.int32)
    lead_val = jax.random.randint(key_lead_val, (groups, NGY, GRP_X), 2, 4, dtype=jnp.int32)
    group_ids = jnp.arange(groups, dtype=jnp.int32)[:, None, None]
    column_ids = jnp.arange(NGY, dtype=jnp.int32)[None, :, None]
    forced_device = (group_ids == forced // NGY) & (column_ids == forced % NGY) & (ranks == 0)
    lead_val = jnp.where(forced_device, ITERS, lead_val)
    atom_ids = jnp.arange(ATOMS, dtype=jnp.int32)
    atom_counts = jnp.where(atom_ids == leading[..., None], lead_val[..., None], base_counts)
    result = jnp.where(slow[..., None], atom_counts, 1)
    result = jnp.transpose(result, (0, 2, 1, 3)).reshape(NGX, NGY, ATOMS)
    return result.astype(jnp.int32)


def touch_ends(values, rng, least, largest):
    spot = [jax.random.randint(jax.random.fold_in(rng, axis), (), 0, length) for axis, length in enumerate(values.shape)]
    widest = values.shape.index(max(values.shape))
    neighbour = spot[:widest] + [(spot[widest] + 1) % values.shape[widest]] + spot[widest + 1:]
    return values.at[tuple(spot)].set(least).at[tuple(neighbour)].set(largest)


def steps_of(rng, shape, split, low, top_value):
    gain, own = 1.0, jax.random.fold_in(rng, 6)
    for dim, parts in split:
        draws = jnp.exp(jax.random.uniform(jax.random.fold_in(own, dim), (parts,), jnp.float32, low / len(split), top_value / len(split)))
        gain = gain * jnp.repeat(draws, shape[dim] // parts).reshape([-1 if axis == dim else 1 for axis in range(len(shape))])
    return gain


def normal_values(own_key, extent, deviation, bound, cuts=(), held_as=jnp.bfloat16):
    array = jax.random.normal(own_key, extent, jnp.float32) * deviation
    if len(cuts) > 0:
        array = steps_of(own_key, extent, cuts, -0.22, 0.18) * array
    return jnp.clip(array, min=-bound, max=bound).astype(held_as)


def setup_inputs(seed: int = 0) -> dict:
    seeds = jax.random.split(jax.random.key(seed), 5)
    blocks = normal_values(seeds[0], (NGX, NGY, OFFSETS, B, B), (81 * B) ** -0.5, 0.0625, ((0, 4), (1, 8)), jnp.float32)
    pair_mask = touch_ends((jax.random.randint(seeds[1], (NGX, NGY, OFFSETS, ATOMS, ATOMS), 0, 4) < 3).astype(jnp.int32), jax.random.fold_in(seeds[1], 1), 0, 1)
    rhs_rows = normal_values(seeds[2], (NGX, NGY, OFFSETS, B, B), 1.0, 6.0, ((0, 4), (1, 8)), jnp.float32)
    counts = draw_counts(jax.random.fold_in(seeds[4], 71), 0)
    return dict(blocks=blocks, pair_mask=pair_mask, rhs_rows=rhs_rows, counts=counts)


def expand_mask(pair_mask, orbitals):
    shaped = pair_mask.astype(jnp.float32)[..., :, None, :, None]
    leading = pair_mask.shape[:-2]
    atom_count = pair_mask.shape[-1]
    expanded = jnp.broadcast_to(shaped, leading + (atom_count, orbitals, atom_count, orbitals))
    return expanded.reshape(leading + (atom_count * orbitals, atom_count * orbitals))

def cluster_apply(window, vectors):
    result = vectors
    for row_off in (-1, 0, 1):
        for col_off in (-1, 0, 1):
            offset = 3 * (row_off + 1) + (col_off + 1)
            row_low, row_high = (max(0, -row_off), min(3, 3 - row_off))
            col_low, col_high = (max(0, -col_off), min(3, 3 - col_off))
            coupled = window[..., row_low:row_high, col_low:col_high, offset, :, :]
            source = vectors[..., row_low + row_off:row_high + row_off, col_low + col_off:col_high + col_off, :, :]
            product = jnp.einsum('...xyij,...xyjc->...xyic', coupled, source, precision=lax.Precision.HIGHEST)
            result = result.at[..., row_low:row_high, col_low:col_high, :, :].add(-product)
    return result

def cluster_rhs(rhs_window):
    rows_list = []
    for row_pos in range(3):
        pieces = []
        for col_pos in range(3):
            pieces.append(rhs_window[..., row_pos, col_pos, 8 - 3 * row_pos - col_pos, :, :])
        rows_list.append(jnp.stack(pieces, axis=-3))
    return jnp.stack(rows_list, axis=-4)

def column_inner(left, other):
    return lax.optimization_barrier(jnp.sum(left * other, axis=(-4, -3, -2)))

def spread(scalar):
    return scalar[..., None, None, None, :]

def guarded(top, bottom, floor_val):
    return top * bottom / (bottom * bottom + floor_val * floor_val)

def start_state(window, right_side):
    image_first = cluster_apply(window, right_side)
    zero_field = jnp.zeros_like(right_side)
    norm_rhs = column_inner(right_side, right_side)
    zero_cols = jnp.zeros_like(norm_rhs)
    vectors = (right_side, right_side, right_side, image_first, image_first, zero_field, zero_field)
    scalars = (norm_rhs, 0.1 * norm_rhs, jnp.sqrt(norm_rhs), zero_cols, zero_cols, norm_rhs)
    return (vectors, scalars)

def iterate(window, vectors, scalars, iteration, limit_cols):
    shadow, residual, first_dir, image_first, vector, direction, solution = vectors
    rho_value, rho_floor, tau_value, theta_value, eta_value, norm_rhs = scalars
    alpha_floor = 0.1 * jnp.sqrt(norm_rhs * (column_inner(vector, vector) + 1e-06))
    alpha_value = guarded(rho_value, column_inner(shadow, vector), alpha_floor)
    step_ratio = guarded(1.0, alpha_value, 0.1)
    second = first_dir - spread(alpha_value) * vector
    image_second = cluster_apply(window, second)
    active = spread((limit_cols > iteration).astype(jnp.float32))
    for half_dir, half_image in ((first_dir, image_first), (second, image_second)):
        residual = residual - spread(alpha_value) * half_image
        direction = half_dir + spread(theta_value * theta_value * eta_value * step_ratio) * direction
        theta_value = jnp.sqrt(column_inner(residual, residual)) / tau_value
        cosine = 1.0 / jnp.sqrt(1.0 + theta_value * theta_value)
        tau_value = tau_value * theta_value * cosine
        eta_value = cosine * cosine * alpha_value
        solution = solution + active * spread(eta_value) * direction
    vectors = (shadow, residual, second, image_second, vector, direction, solution)
    scalars = (rho_value, rho_floor, tau_value, theta_value, eta_value, norm_rhs)
    return (vectors, scalars)

def advance(window, vectors, scalars):
    shadow, residual, second, image_second, vector, direction, solution = vectors
    rho_value, rho_floor, tau_value, theta_value, eta_value, norm_rhs = scalars
    rho_next = column_inner(shadow, residual)
    beta_value = guarded(rho_next, rho_value, rho_floor)
    next_floor = 0.1 * jnp.sqrt(norm_rhs * column_inner(residual, residual))
    first_dir = residual + spread(beta_value) * second
    image_first = cluster_apply(window, first_dir)
    vector = image_first + spread(beta_value) * (image_second + spread(beta_value) * vector)
    vectors = (shadow, residual, first_dir, image_first, vector, direction, solution)
    scalars = (rho_next, next_floor, tau_value, theta_value, eta_value, norm_rhs)
    return (vectors, scalars)

def first_section(window, right_side, limit_cols):
    vectors, scalars = start_state(window, right_side)
    return iterate(window, vectors, scalars, 0, limit_cols)

def later_section(window, vectors, scalars, limit_cols):
    for iteration in range(1, ITERS):
        vectors, scalars = advance(window, vectors, scalars)
        vectors, scalars = iterate(window, vectors, scalars, iteration, limit_cols)
    return vectors[6]

def reference(blocks, pair_mask, rhs_rows, counts):
    coupling = blocks * expand_mask(pair_mask, ORB)
    widths = ((1, 1), (1, 1), (0, 0), (0, 0), (0, 0))
    padded_coupling = jnp.pad(coupling, widths)
    padded_rhs = jnp.pad(rhs_rows, widths)
    limits = jnp.repeat(counts, ORB, axis=-1).astype(jnp.float32)

    def one_group(block_index):
        zero_idx = jnp.zeros((), jnp.int32)
        first_pos = (block_index // NGY).astype(jnp.int32)
        second_pos = (block_index % NGY).astype(jnp.int32)
        starts = (first_pos, second_pos, zero_idx, zero_idx, zero_idx)
        window = lax.dynamic_slice(padded_coupling, starts, (3, 3, OFFSETS, B, B))
        rhs_window = lax.dynamic_slice(padded_rhs, starts, (3, 3, OFFSETS, B, B))
        limit_cols = lax.dynamic_slice(limits, (first_pos, second_pos, zero_idx), (1, 1, B)).reshape(B)
        vectors, scalars = first_section(window, cluster_rhs(rhs_window), limit_cols)
        return later_section(window, vectors, scalars, limit_cols)
    result = lax.map(one_group, jnp.arange(NGX * NGY, dtype=jnp.int32))
    return result.reshape(NGX, NGY, OFFSETS, B, B)
```

```python
import jax
import jax.numpy as jnp
from jax import lax
from jax.experimental import pallas as pl
from jax.experimental.pallas import tpu as pltpu
from jax.sharding import PartitionSpec as P

ITERS = 3
MESH = pl.DeviceIdType.MESH
F32 = jnp.float32
BF16 = jnp.bfloat16


def guarded(top, bottom, floor_val):
    return top * bottom / (bottom * bottom + floor_val * floor_val)


def split(value):
    high = value.astype(BF16)
    return high, (value - high.astype(F32)).astype(BF16)


def product(left, right):
    return jnp.dot(left, right, preferred_element_type=F32)


ROW_OF = (1, 0)
OU_OF = (1, 0)
EDGE = (2, 0)
PAIRS = ((0, 0, 1, 0), (0, 1, 2, -1), (1, 0, 0, 1), (1, 1, 1, 0))


def sources(s):
    return range(max(0, s - 1), min(3, s + 2))


def kernel(
    blocks, masks, rhs, limits, own_masks, out,
    own_c, g_c, n_c0, n_c1, f_c0, f_c1, d_c, passing,
    o_r, g_r, n_r, f_r, d_r, n_m, f_m, g_m, d_m, own_w,
    shared, single0, single1, single2, single3, vec, basis,
    send_sem, recv_sem, local_sem,
):
    b = blocks.shape[-1]
    atoms = masks.shape[-1]
    orb = b // atoms
    gx, gy = lax.axis_index("gx"), lax.axis_index("gy")
    ngx, ngy = lax.axis_size("gx"), lax.axis_size("gy")
    assert ngy % 2 == 0
    half = ngy // 2
    odd = gy % 2
    sign = 1 - 2 * odd
    gx_to = (gx < ngx - 1, gx > 0)
    gx_from = (gx > 0, gx < ngx - 1)
    gx_dev = ((gx + 1, gy), (gx - 1, gy))
    near_dev, far_dev, hop_dev = (gx, gy + sign), (gx, gy - sign), (gx, gy + 2 * sign)

    def inside(index):
        return jnp.logical_and(index >= 0, index < ngy)

    has_far = inside(gy - sign)
    has_hop = inside(gy + 2 * sign)
    place_in = gy // 2
    rank = jnp.where(odd == 0, place_in, half - 1 - place_in)
    mine_relayed = (4 * rank) // half
    partner_relayed = (4 * (half - 1 - rank)) // half

    def turned(k):
        return 1 if k == 1 else 2 * odd + sign * k

    numbers = {}

    def number(kind, name):
        return numbers.setdefault((kind, name), sum(1 for key in numbers if key[0] == kind))

    def remote(src, dst, device, name, arrival=None):
        return pltpu.make_async_remote_copy(
            src_ref=src, dst_ref=dst, send_sem=send_sem.at[number("send", name)],
            recv_sem=recv_sem.at[number("recv", arrival or name)],
            device_id=device, device_id_type=MESH,
        )

    far_groups = []
    for i in range(4):
        row = i % 2
        source, target = ((rhs, f_r), (blocks, f_c1))[i // 2]
        far_groups.append((source.at[row, :, turned(0)], target.at[row]))
    far_direct = [remote(src, dst, far_dev, ("fd", i), ("fg", i))
                  for i, (src, dst) in enumerate(far_groups)]
    far_pass = [remote(src, passing.at[i], near_dev, ("fp", i))
                for i, (src, _) in enumerate(far_groups)]
    far_hop = [remote(passing.at[i], dst, hop_dev, ("fh", i), ("fg", i))
               for i, (_, dst) in enumerate(far_groups)]
    near_mask = [remote(masks.at[:, :, turned(1 + k)], n_m.at[:, :, k], near_dev, ("nm", k))
                 for k in (0, 1)]
    far_mask = [remote(masks.at[:, :, turned(1 - k)], f_m.at[:, :, k], far_dev, ("fm", k))
                for k in (0, 1)]
    near_c0 = [remote(blocks.at[row, :, 1], n_c0.at[row], near_dev, ("n0", row)) for row in (0, 1)]
    far_c0 = [remote(n_c0.at[row], f_c0.at[row], hop_dev, ("f0", row)) for row in (0, 1)]
    near_rd, near_rn, near_1d, near_1n = [], [], [], []
    for h in (0, 1):
        row, ou, edge = ROW_OF[h], OU_OF[h], EDGE[h]
        two, rest, other = pl.ds(ou, 2), 2 - edge, pl.ds(1 - ou, 2)
        near_rd.append(remote(
            rhs.at[row, edge, turned(2)], n_r.at[row, edge], near_dev, ("rd", h)))
        near_rn.append(remote(
            rhs.at[row, other, turned(2)], n_r.at[row, other], near_dev, ("rn", h)))
        near_1d.append(remote(
            blocks.at[row, two, turned(2)], n_c1.at[row, two], near_dev, ("1d", h)))
        near_1n.append(remote(
            blocks.at[row, rest, turned(2)], n_c1.at[row, rest], near_dev, ("1n", h)))
    gx_direct, diag = [], {}
    for h in (0, 1):
        row, two, edge = ROW_OF[h], pl.ds(OU_OF[h], 2), EDGE[h]
        gx_direct.append([
            remote(masks.at[row, two], g_m.at[h], gx_dev[h], ("gm", h)),
            remote(rhs.at[row, edge, 1], g_r.at[h], gx_dev[h], ("gr", h)),
            remote(blocks.at[row, two], g_c.at[h], gx_dev[h], ("gc", h)),
        ])
        for side, (m, r, c0, c1) in enumerate(((n_m, n_r, n_c0, n_c1), (f_m, f_r, f_c0, f_c1))):
            diag[h, side] = [
                remote(m.at[row, two], d_m.at[h, side], gx_dev[h], ("dm", h, side)),
                remote(r.at[row, edge], d_r.at[h, side], gx_dev[h], ("dr", h, side)),
                remote(c0.at[row, two], d_c.at[h, side, 0], gx_dev[h], ("d0", h, side)),
                remote(c1.at[row, two], d_c.at[h, side, 1], gx_dev[h], ("d1", h, side)),
            ]

    barrier = pltpu.get_barrier_semaphore()
    total = jnp.int32(0)
    peers = [(gx_to[h], gx_dev[h]) for h in (0, 1)]
    peers += [(inside(gy + step), (gx, gy + step)) for step in (-2, -1, 1, 2)]
    for exists, device in peers:
        total = total + exists.astype(jnp.int32)

        @pl.when(exists)
        def _(device=device):
            pl.semaphore_signal(barrier, inc=1, device_id=device, device_id_type=MESH)
    pl.semaphore_wait(barrier, total)

    def start(condition, copies):
        @pl.when(condition)
        def _():
            for copy in copies:
                copy.start()

    def arrived(condition, copies, absent=()):
        @pl.when(condition)
        def _():
            for copy in copies:
                copy.wait_recv()

        if absent:
            @pl.when(jnp.logical_not(condition))
            def _():
                for ref in absent:
                    ref[...] = jnp.zeros(ref.shape, ref.dtype)

    both = jnp.logical_and
    for copy in near_mask:
        copy.start()
    start(has_far, far_mask)
    for i in range(4):
        start(both(has_far, i < mine_relayed), [far_pass[i]])
        start(both(has_far, i >= mine_relayed), [far_direct[i]])
    for copy in near_c0 + near_rd + near_rn + near_1d + near_1n:
        copy.start()
    for h in (0, 1):
        start(gx_to[h], gx_direct[h])

    local_c = pltpu.make_async_copy(blocks, own_c, local_sem.at[0])
    local_r = [pltpu.make_async_copy(rhs.at[row, ou, 1], o_r.at[k], local_sem.at[1 + k])
               for k, (row, _, ou, _) in enumerate(PAIRS)]
    for copy in [local_c] + local_r:
        copy.start()

    spread = (
        lax.broadcasted_iota(jnp.int32, (atoms, b), 1) // orb
        == lax.broadcasted_iota(jnp.int32, (atoms, b), 0)
    ).astype(F32)

    def widen(value):
        flat = value.astype(F32).reshape(-1, atoms)
        wide = jnp.dot(flat, spread, preferred_element_type=F32)
        return wide.reshape(value.shape[:-1] + (b,))

    def put(w, s, ou, ov, value, mask):
        masked = (value.reshape(b // orb, orb, b) * mask[:, None, :]).reshape(b, b)
        from_w, at = w + ou - 1, s + ov - 1 - sources(s)[0]
        first = 0
        if w in (1, 2) and from_w in (1, 2):
            ref, first, col = shared, b * (w - 1), 2 * at + from_w - 1
        elif w == 0:
            ref, col = single0, 2 * at + from_w
        elif w == 3:
            ref, col = single3, 2 * at + from_w - 2
        else:
            ref, col = (single1 if w == 1 else single2), at
        for part, piece in enumerate(split(masked)):
            ref[s, part, first:first + b, b * col:b * col + b] = piece

    def put_rhs(group, u, s, value):
        basis[0, b * (3 * s + u):b * (3 * s + u) + b, b * group:b * group + b] = value
        at = b * (4 * s + u + group)
        for part, piece in enumerate(split(value)):
            vec[0, part, at:at + b, b * group:b * group + b] = piece

    local_c.wait()
    own_w[...] = widen(own_masks[...])
    for row in (0, 1):
        for ou in range(3):
            for ov in range(3):
                put(row + 1, 1, ou, ov, own_c[row, ou, turned(ov)], own_w[row, ou, turned(ov)])
    for k, (row, group, ou, off) in enumerate(PAIRS):
        local_r[k].wait()
        put_rhs(group, off + 1, 1, o_r[k])

    for h in (0, 1):
        arrived(gx_from[h], gx_direct[h], [g_m.at[h], g_r.at[h], g_c.at[h]])
        own_w[h, 0:2] = widen(g_m[h])
        for ou in range(2):
            for ov in range(3):
                put(3 * h, 1, ou + OU_OF[h], ov, g_c[h, ou, turned(ov)], own_w[h, ou, turned(ov)])
        put_rhs(h, 2 * h, 1, g_r[h])

    for k in (0, 1):
        near_mask[k].wait_recv()
    for h in (0, 1):
        start(gx_to[h], diag[h, 0][0:1])
    for i in range(4):
        @pl.when(i < partner_relayed)
        def _(i=i):
            far_pass[i].wait_recv()
            far_hop[i].start()
    n_wide = widen(n_m[...])
    for h in (1, 0):
        row = ROW_OF[h]
        near_c0[row].wait_recv()
        start(has_hop, [far_c0[row]])
        start(gx_to[h], diag[h, 0][2:3])
        for ou in range(3):
            put(row + 1, 2, ou, 1, n_c0[row, ou], n_wide[row, ou, 0])
    arrived(has_far, far_mask, [f_m])
    for h in (0, 1):
        start(both(has_far, gx_to[h]), diag[h, 1][0:1])
    f_wide = widen(f_m[...])
    for row in (0, 1):
        arrived(has_far, [far_direct[row]], [f_r.at[row]])
        h = 1 - row
        start(both(has_far, gx_to[h]), diag[h, 1][1:2])
    for h in (0, 1):
        near_rd[h].wait_recv()
        start(gx_to[h], diag[h, 0][1:2])
    for row in (0, 1):
        arrived(has_far, [far_direct[2 + row]], [f_c1.at[row]])
        h = 1 - row
        start(both(has_far, gx_to[h]), diag[h, 1][3:4])
        for ou in range(3):
            put(row + 1, 0, ou, 2, f_c1[row, ou], f_wide[row, ou, 1])
    for row in (0, 1):
        arrived(has_far, [far_c0[row]], [f_c0.at[row]])
        h = 1 - row
        start(both(has_far, gx_to[h]), diag[h, 1][2:3])
        for ou in range(3):
            put(row + 1, 0, ou, 1, f_c0[row, ou], f_wide[row, ou, 0])
    for h in (0, 1):
        near_rn[h].wait_recv()
    for row, group, ou, off in PAIRS:
        put_rhs(group, off + 1, 2, n_r[row, ou])
        put_rhs(group, off + 1, 0, f_r[row, ou])
    for h in (0, 1):
        near_1d[h].wait_recv()
        start(gx_to[h], diag[h, 0][3:4])
    for h in (0, 1):
        row = ROW_OF[h]
        for ou in (OU_OF[h], OU_OF[h] + 1):
            put(row + 1, 2, ou, 0, n_c1[row, ou], n_wide[row, ou, 1])

    def corner(h, side):
        arrived(gx_from[h] if side == 0 else both(gx_from[h], has_far), diag[h, side],
                [d_m.at[h, side], d_r.at[h, side], d_c.at[h, side]])
        wide = widen(d_m[h, side])
        s = 2 - 2 * side
        for k in (0, 1):
            for ou in range(2):
                put(3 * h, s, ou + OU_OF[h], 1 if k == 0 else 2 * side,
                    d_c[h, side, k, ou], wide[ou, k])
        put_rhs(h, 2 * h, s, d_r[h, side])

    for side in (1, 0):
        for h in (0, 1):
            corner(h, side)
    for h in (0, 1):
        near_1n[h].wait_recv()
        row, ou = ROW_OF[h], 2 - EDGE[h]
        put(row + 1, 2, ou, 0, n_c1[row, ou], n_wide[row, ou, 1])

    def fold(value):
        return jnp.sum(value.reshape(-1, 8, 2 * b), axis=0)

    def column(value):
        return jnp.sum(value, axis=0, keepdims=True)

    def at_of(s, u):
        return pl.ds(b * (3 * s + u), b)

    def apply_rows(turn, s):
        count = len(sources(s))

        def tall(part, w, strips, lanes):
            return jnp.concatenate(
                [vec[turn, part, b * (4 * k + w):b * (4 * k + w + strips), lanes] for k in sources(s)],
                axis=0)

        every = slice(0, 2 * b)
        high, low = tall(0, 1, 2, every), tall(1, 1, 2, every)
        c_high = shared[s, 0, :, 0:2 * b * count]
        c_low = shared[s, 1, :, 0:2 * b * count]
        joint = product(
            jnp.concatenate([c_high, c_low, c_high], axis=1),
            jnp.concatenate([high, high, low], axis=0))

        def alone(ref, w, strips, group):
            lanes = slice(b * group, b * group + b)
            right = jnp.concatenate([tall(0, w, strips, lanes), tall(1, w, strips, lanes)], axis=1)
            width = b * strips * count
            left = jnp.concatenate([ref[s, 0, :, 0:width], ref[s, 1, :, 0:width]], axis=1)
            value = product(left, jnp.concatenate([right, right], axis=0))
            return value[:, 0:b] + value[:, b:2 * b]

        first, second = joint[0:b], joint[b:2 * b]
        return (
            jnp.concatenate([alone(single0, 0, 2, 0), first[:, b:]], axis=1),
            jnp.concatenate([first[:, 0:b] + alone(single1, 0, 1, 0),
                             second[:, b:] + alone(single2, 3, 1, 1)], axis=1),
            jnp.concatenate([second[:, 0:b], alone(single3, 2, 2, 1)], axis=1),
        )

    gram = {}

    def power(j):
        sums = [jnp.zeros((8, 2 * b), F32) for _ in range(j + 1)]
        for s in (1, 0, 2):
            for u, value in enumerate(apply_rows((j - 1) % 2, s)):
                basis[j, at_of(s, u), :] = value
                for part, piece in enumerate(split(value)):
                    for group in (0, 1):
                        at = b * (4 * s + u + group)
                        vec[j % 2, part, at:at + b, b * group:b * group + b] = (
                            piece[:, b * group:b * group + b])
                for i in range(j):
                    sums[i] = sums[i] + fold(value * basis[i, at_of(s, u), :])
                sums[j] = sums[j] + fold(value * value)
        for i in range(j + 1):
            gram[i, j] = gram[j, i] = column(sums[i])

    def add(left, factor, right):
        size = max(len(left), len(right))
        result = []
        for k in range(size):
            a = left[k] if k < len(left) else None
            c = right[k] if k < len(right) else None
            if c is None:
                result.append(a)
            else:
                result.append(factor * c if a is None else a + factor * c)
        return result

    def image(value):
        return add(list(value) + [None], -1.0, [None] + list(value))

    def inner(left, other):
        result = None
        for i, a in enumerate(left):
            for k, c in enumerate(other):
                if a is None or c is None:
                    continue
                term = (a * c) * gram[i, k]
                result = term if result is None else result + term
        return result

    def norm_of(value):
        result = None
        for i, a in enumerate(value):
            for k in range(i, len(value)):
                term = (a * value[k]) * gram[i, k] * (1.0 if i == k else 2.0)
                result = term if result is None else result + term
        return jnp.maximum(result, 0.0)

    start_sums = jnp.zeros((8, 2 * b), F32)
    for s in range(3):
        for u in range(3):
            value = basis[0, at_of(s, u), :]
            start_sums = start_sums + fold(value * value)
    gram[0, 0] = column(start_sums)
    limit = jnp.concatenate(
        [widen(jnp.broadcast_to(limits[group], (atoms, atoms)))[0:1] for group in (0, 1)], axis=1)

    power(1)
    norm = gram[0, 0]
    one = jnp.ones_like(norm)
    shadow = [one]
    resid = [one]
    y_first = [one]
    rho, floor = norm, 0.1 * norm
    tau = jnp.sqrt(norm)
    theta = eta = jnp.zeros_like(norm)
    u_first = image(y_first)
    along = u_first
    direc, sol = [], []
    y_second = u_second = None
    for n in range(1, ITERS + 1):
        active = (limit >= float(n)).astype(F32)
        if n > 1:
            power(2 * n - 1)
            rho_next = inner(shadow, resid)
            beta = guarded(rho_next, rho, floor)
            floor = 0.1 * jnp.sqrt(norm * size)
            rho = rho_next
            y_first = add(resid, beta, y_second)
            u_first = image(y_first)
            along = add(u_first, beta, add(u_second, beta, along))
        alpha = guarded(rho, inner(shadow, along), 0.1 * jnp.sqrt(norm * (norm_of(along) + 1e-06)))
        ratio = guarded(1.0, alpha, 0.1)
        y_second = add(y_first, -alpha, along)
        u_second = image(y_second)
        for part, (y, u) in enumerate(((y_first, u_first), (y_second, u_second))):
            resid = add(resid, -alpha, u)
            direc = add(y, theta * theta * eta * ratio, direc)
            if part == 1 and n < ITERS:
                power(2 * n)
            if part == 1 and n == ITERS:
                sums = jnp.zeros((8, 2 * b), F32)
                for s in (1, 0, 2):
                    for r, value in enumerate(apply_rows((2 * n - 1) % 2, s)):
                        value = value * resid[2 * n]
                        for i in range(2 * n):
                            value = value + basis[i, at_of(s, r), :] * resid[i]
                        sums = sums + fold(value * value)
                size = column(sums)
            else:
                size = norm_of(resid)
            theta = jnp.sqrt(size) / tau
            cosine = 1.0 / jnp.sqrt(1.0 + theta * theta)
            tau = tau * theta * cosine
            eta = cosine * cosine * alpha
            sol = add(sol, active * eta, direc)

    for s in range(3):
        for u in range(3):
            value = basis[0, at_of(s, u), :] * sol[0]
            for i in range(1, 2 * ITERS):
                value = value + basis[i, at_of(s, u), :] * sol[i]
            for group in (0, 1):
                out[group, 3 * u + turned(s)] = value[:, b * group:b * group + b]

    for copy in near_mask + near_c0 + near_rd + near_rn + near_1d + near_1n:
        copy.wait_send()

    def sent(condition, copies):
        @pl.when(condition)
        def _():
            for copy in copies:
                copy.wait_send()

    sent(has_far, far_mask)
    sent(has_hop, far_c0)
    for i in range(4):
        sent(both(has_far, i < mine_relayed), [far_pass[i]])
        sent(both(has_far, i >= mine_relayed), [far_direct[i]])
        sent(i < partner_relayed, [far_hop[i]])
    for h in (0, 1):
        sent(gx_to[h], gx_direct[h] + diag[h, 0])
        sent(both(gx_to[h], has_far), diag[h, 1])
    assert len(numbers) <= 2 * COPIES


COPIES = 56


def shards(blocks, pair_mask, rhs_rows, counts):
    groups = blocks.shape[0]
    b = blocks.shape[-1]
    atoms = pair_mask.shape[-1]
    blocks = blocks.reshape(groups, 3, 3, b, b)
    rhs = rhs_rows.reshape(groups, 3, 3, b, b)
    masks = pair_mask.reshape(groups, 3, 3, atoms, atoms)
    any_spec = pl.BlockSpec(memory_space=pl.ANY)
    vmem_spec = pl.BlockSpec(memory_space=pltpu.VMEM)

    def raw(*lead):
        return pltpu.VMEM(lead + (b, b), F32)

    def flags(*lead):
        return pltpu.VMEM(lead + (atoms, atoms), jnp.int32)

    solved = pl.pallas_call(
        kernel,
        out_shape=pltpu.VMEM((groups, 9, b, b), F32),
        in_specs=[any_spec, any_spec, any_spec, vmem_spec, vmem_spec],
        out_specs=vmem_spec,
        scratch_shapes=[
            raw(groups, 3, 3), raw(2, 2, 3), raw(groups, 3), raw(groups, 3), raw(groups, 3),
            raw(groups, 3), raw(2, 2, 2, 2), raw(4, 3),
            raw(4), raw(2), raw(groups, 3), raw(groups, 3), raw(2, 2),
            flags(groups, 3, 2), flags(groups, 3, 2), flags(2, 2, 3), flags(2, 2, 2, 2),
            pltpu.VMEM((groups, 3, 3, atoms, b), F32),
            pltpu.VMEM((3, 2, 2 * b, 6 * b), BF16),
            pltpu.VMEM((3, 2, b, 6 * b), BF16),
            pltpu.VMEM((3, 2, b, 3 * b), BF16),
            pltpu.VMEM((3, 2, b, 3 * b), BF16),
            pltpu.VMEM((3, 2, b, 6 * b), BF16),
            pltpu.VMEM((2, 2, 12 * b, 2 * b), BF16),
            pltpu.VMEM((2 * ITERS, 9 * b, 2 * b), F32),
            pltpu.SemaphoreType.DMA((COPIES,)),
            pltpu.SemaphoreType.DMA((COPIES,)),
            pltpu.SemaphoreType.DMA((5,)),
        ],
        compiler_params=pltpu.CompilerParams(
            collective_id=0, has_side_effects=True, vmem_limit_bytes=60 * 1024 * 1024
        ),
    )(blocks, masks, rhs, counts, masks)
    return solved.reshape(groups, 1, 9, b, b)


def solution(mesh):
    spec = P("gx", "gy", None, None, None)
    return jax.shard_map(
        shards,
        mesh=mesh,
        in_specs=(spec, spec, spec, P("gx", "gy", None)),
        out_specs=spec,
        check_vma=False,
    )
```

```python
import jax
import jax.numpy as jnp
from jax import lax
from jax.experimental import pallas as pl
from jax.experimental.pallas import tpu as pltpu
from jax.sharding import PartitionSpec as P

ITERS = 3
COPIES = 80
MESH = pl.DeviceIdType.MESH
F32 = jnp.float32
BF16 = jnp.bfloat16


def guarded(top, bottom, floor_val):
    return top * bottom / (bottom * bottom + floor_val * floor_val)


def split(value):
    high = value.astype(BF16)
    return high, (value - high.astype(F32)).astype(BF16)


def product(left, right):
    return jnp.dot(left, right, preferred_element_type=F32)


def near_three(s):
    return range(max(0, s - 1), min(3, s + 2))


def add(left, factor, right):
    result = []
    for k in range(max(len(left), len(right))):
        a = left[k] if k < len(left) else None
        c = right[k] if k < len(right) else None
        if c is None:
            result.append(a)
        else:
            result.append(factor * c if a is None else a + factor * c)
    return result


def image(value):
    return add(list(value) + [None], -1.0, [None] + list(value))


def kernel(
    blocks, masks, rhs, limits, own_masks, out,
    own_c, g_c, n_c0, n_c1, f_c0, f_c1, d_c, passing,
    o_r, g_r, n_r, f_r, d_r, n_m, f_m, g_m, d_m, wide,
    c_of0, c_of1, c_of2, c_of3, vec, basis,
    send_sem, recv_sem, local_sem,
):
    b = blocks.shape[-1]
    atoms = masks.shape[1]
    offsets = masks.shape[-1]
    orb = b // atoms
    gx, gy = lax.axis_index("gx"), lax.axis_index("gy")
    ngx, ngy = lax.axis_size("gx"), lax.axis_size("gy")
    assert ngx % 2 == 0 and ngy % 2 == 0
    half = ngy // 2
    core, odd = gx % 2, gy % 2
    step_x, step_y = 1 - 2 * core, 1 - 2 * odd
    inner_dev, outer_dev = (gx + step_x, gy), (gx - step_x, gy)
    near_dev, far_dev, hop_dev = (gx, gy + step_y), (gx, gy - step_y), (gx, gy + 2 * step_y)

    def inside(index, size):
        return jnp.logical_and(index >= 0, index < size)

    both = jnp.logical_and
    has_outer = inside(gx - step_x, ngx)
    has_far = inside(gy - step_y, ngy)
    has_hop = inside(gy + 2 * step_y, ngy)
    side_there = (None, has_far)
    rank = jnp.where(odd == 0, gy // 2, half - 1 - gy // 2)
    mine_relayed = (4 * rank) // half
    partner_relayed = (4 * (half - 1 - rank)) // half

    def ty(j):
        return 1 if j == 1 else 2 * odd + step_y * j

    def tx(k):
        return 1 if k == 1 else 2 * (1 - core) - step_x * k

    rows = (1 - core, core)
    head, tail = pl.ds(1 - core, 2), pl.ds(core, 2)
    full = pl.ds(0, 3)

    numbers = {}

    def number(kind, name):
        return numbers.setdefault((kind, name), sum(1 for key in numbers if key[0] == kind))

    def remote(src, dst, device, name, arrival=None):
        return pltpu.make_async_remote_copy(
            src_ref=src, dst_ref=dst, send_sem=send_sem.at[number("send", name)],
            recv_sem=recv_sem.at[number("recv", arrival or name)],
            device_id=device, device_id_type=MESH,
        )

    n_mask = remote(masks, n_m, near_dev, "nm")
    f_mask = remote(n_m, f_m, hop_dev, "fm")
    far_parts = (
        (0, rhs, f_r, rows[0], head, (0, 2)), (0, rhs, f_r, rows[1], pl.ds(tx(0), 1), (2, 1)),
        (1, blocks, f_c1, rows[0], full, (3, 3)),
        (2, rhs, f_r, rows[1], tail, (6, 2)), (2, rhs, f_r, rows[0], pl.ds(tx(2), 1), (8, 1)),
        (4, blocks, f_c1, rows[1], head, None), (4, blocks, f_c1, rows[1], pl.ds(tx(2), 1), None),
    )
    far_direct, far_pass, far_hop, far_group = [], [], [], []
    for i, (group, source, target, row, ous, slot) in enumerate(far_parts):
        src, dst = source.at[row, ous, ty(0)], target.at[row, ous]
        far_group.append(group)
        far_direct.append(remote(src, dst, far_dev, ("fd", i), ("fg", i)))
        if slot is not None:
            held = passing.at[pl.ds(*slot)]
            far_pass.append(remote(src, held, near_dev, ("fp", i)))
            far_hop.append(remote(held, dst, hop_dev, ("fh", i), ("fg", i)))

    c_parts = ((rows[0], full), (rows[1], head), (rows[1], pl.ds(tx(2), 1)))
    near_c0 = [remote(blocks.at[row, ous, 1], n_c0.at[row, ous], near_dev, ("n0", i))
               for i, (row, ous) in enumerate(c_parts)]
    near_c1 = [remote(blocks.at[row, ous, ty(2)], n_c1.at[row, ous], near_dev, ("n1", i))
               for i, (row, ous) in enumerate(c_parts)]
    far_c0 = [remote(n_c0.at[row, ous], f_c0.at[row, ous], hop_dev, ("f0", i))
              for i, (row, ous) in enumerate(c_parts)]
    near_r = [remote(rhs.at[row, ous, ty(2)], n_r.at[row, ous], near_dev, ("nr", i))
              for i, (row, ous) in enumerate((
                  (rows[0], head), (rows[1], pl.ds(tx(0), 1)),
                  (rows[1], tail), (rows[0], pl.ds(tx(2), 1))))]

    direct_in = [
        remote(masks.at[rows[0]], g_m.at[0], inner_dev, "gm0"),
        remote(rhs.at[rows[0], tx(0), 1], g_r.at[0], inner_dev, "gr0"),
        remote(blocks.at[rows[0], head], g_c.at[0], inner_dev, "gc0"),
    ]
    direct_out = [
        remote(masks.at[rows[1]], g_m.at[1], outer_dev, "gm1"),
        remote(rhs.at[rows[1], tx(2), 1], g_r.at[1], outer_dev, "gr1"),
        remote(blocks.at[rows[1], tail], g_c.at[1], outer_dev, "gc1"),
    ]
    in_m, in_r, in_c, out_m, out_r, out_mid, out_end = [], [], [], [], [], [], []
    for side, (m, r, coupled) in enumerate(((n_m, n_r, (n_c0, n_c1)), (f_m, f_r, (f_c0, f_c1)))):
        in_m.append(remote(m.at[rows[0]], d_m.at[0, side], inner_dev, ("im", side)))
        in_r.append(remote(r.at[rows[0], tx(0)], d_r.at[0, side], inner_dev, ("ir", side)))
        out_m.append(remote(m.at[rows[1]], d_m.at[1, side], outer_dev, ("om", side)))
        out_r.append(remote(r.at[rows[1], tx(2)], d_r.at[1, side], outer_dev, ("or", side)))
        in_c.append([remote(c.at[rows[0], head], d_c.at[0, side, k], inner_dev, ("ic", side, k))
                     for k, c in enumerate(coupled)])
        out_mid.append([remote(c.at[rows[1], 1], d_c.at[1, side, k, 1 - core], outer_dev, ("oc", side, k))
                        for k, c in enumerate(coupled)])
        out_end.append([remote(c.at[rows[1], tx(2)], d_c.at[1, side, k, core], outer_dev, ("oe", side, k))
                        for k, c in enumerate(coupled)])

    barrier = pltpu.get_barrier_semaphore()
    total = jnp.int32(0)
    peers = [(inside(gx + step, ngx), (gx + step, gy)) for step in (-1, 1)]
    peers += [(inside(gy + step, ngy), (gx, gy + step)) for step in (-2, -1, 1, 2)]
    for exists, device in peers:
        total = total + exists.astype(jnp.int32)

        @pl.when(exists)
        def _(device=device):
            pl.semaphore_signal(barrier, inc=1, device_id=device, device_id_type=MESH)
    pl.semaphore_wait(barrier, total)

    def on(condition, actions):
        if condition is None:
            for action in actions:
                action()
        else:
            @pl.when(condition)
            def _():
                for action in actions:
                    action()

    def start(condition, *copies):
        on(condition, [copy.start for copy in copies])

    def arrived(condition, *copies):
        on(condition, [copy.wait_recv for copy in copies])

    def sent(condition, *copies):
        on(condition, [copy.wait_send for copy in copies])

    def is_relayed(i):
        return far_group[i] < mine_relayed

    def start_pass(group):
        for i, copy in enumerate(far_pass):
            if far_group[i] == group:
                start(is_relayed(i), copy)

    def start_direct(i):
        start(both(has_far, jnp.logical_not(is_relayed(i))), far_direct[i])

    def relay(group):
        for i, copy in enumerate(far_pass):
            if far_group[i] == group:
                @pl.when(group < partner_relayed)
                def _(i=i, copy=copy):
                    copy.wait_recv()
                    far_hop[i].start()

    n_mask.start()
    start_pass(0)
    start(None, near_c0[0], near_c0[1])
    start_pass(1)
    start(None, near_r[0], near_r[1], near_c1[0], near_c1[1])
    for i in (0, 1, 2, 5):
        start_direct(i)
    start(None, *direct_in)
    start(has_outer, *direct_out)
    start_pass(2)
    start(None, near_c0[2], near_c1[2], near_r[2], near_r[3])
    for i in (6, 3, 4):
        start_direct(i)

    local_c = pltpu.make_async_copy(blocks, own_c, local_sem.at[0])
    own_rhs = ((0, 1, 0, 1), (0, 2, 1, 0), (1, 0, 0, 2), (1, 1, 1, 1))
    local_r = [pltpu.make_async_copy(rhs.at[rows[t], tx(k), 1], o_r.at[i], local_sem.at[1 + i])
               for i, (_, _, t, k) in enumerate(own_rhs)]
    start(None, local_c, *local_r)

    def clear(*refs):
        for ref in refs:
            ref[...] = jnp.zeros(ref.shape, ref.dtype)

    @pl.when(jnp.logical_not(has_far))
    def _():
        clear(f_c0, f_c1, f_r, f_m, *[d.at[x, 1] for d in (d_c, d_r, d_m) for x in (0, 1)])

    @pl.when(jnp.logical_not(has_outer))
    def _():
        clear(g_c.at[1], g_r.at[1], g_m.at[1], d_c.at[1], d_r.at[1], d_m.at[1])

    wide_shape = (atoms * atoms, atoms * b)
    above, across = (lax.broadcasted_iota(jnp.int32, wide_shape, d) for d in (0, 1))
    spread = (above == atoms * (across // b) + across % b // orb).astype(F32)

    def widen(index, value):
        flat = value.astype(F32).reshape(atoms * atoms, offsets)
        wide[index] = lax.dot_general(
            flat, spread, (((0,), (0,)), ((), ())), preferred_element_type=F32)

    c_refs = (c_of0, c_of1, c_of2, c_of3)
    first_row = (0, 0, 1, 2)

    def put(w, s, k, j, value, mask):
        mask_row = wide[mask, pl.ds(3 * tx(k) + ty(j), 1), :]
        found = near_three(s)
        col = b * ((w + k - 1 - first_row[w]) * len(found) + s + j - 1 - found[0])
        for i in range(atoms):
            masked = value[orb * i:orb * (i + 1)] * mask_row[:, b * i:b * (i + 1)]
            for part, piece in enumerate(split(masked)):
                at = b * part + orb * i
                c_refs[w][s, at:at + orb, col:col + b] = piece

    def put_rhs(solve, u, s, value):
        at = b * (3 * u + s)
        basis[solve, 0, at:at + b, :] = value
        for part, piece in enumerate(split(value)):
            vec[solve, 0, at:at + b, b * part:b * part + b] = piece

    local_c.wait()
    for row in (0, 1):
        widen(row, own_masks[row])
    for t in (0, 1):
        for k in range(3):
            for j in range(3):
                put(1 + t, 1, k, j, own_c[rows[t], tx(k), ty(j)], rows[t])
    for i, (solve, u, _, _) in enumerate(own_rhs):
        local_r[i].wait()
        put_rhs(solve, u, 1, o_r[i])

    arrived(None, *direct_in)
    widen(2, g_m[0])
    for k, slot in ((1, 1 - core), (2, core)):
        for j in range(3):
            put(0, 1, k, j, g_c[0, slot, ty(j)], 2)
    put_rhs(0, 0, 1, g_r[0])

    n_mask.wait_recv()
    start(has_hop, f_mask)
    start(None, in_m[0])
    start(has_outer, out_m[0])
    relay(0)
    for row in (0, 1):
        widen(4 + row, n_m[row])

    def put_column(s, ref, t, k, j):
        put(1 + t, s, k, j, ref[rows[t], tx(k)], (4 if s == 2 else 6) + rows[t])

    near_c0[0].wait_recv()
    start(has_hop, far_c0[0])
    start(None, in_c[0][0])
    for k in range(3):
        put_column(2, n_c0, 0, k, 1)
    near_c0[1].wait_recv()
    start(has_hop, far_c0[1])
    start(has_outer, out_mid[0][0])
    for k in (0, 1):
        put_column(2, n_c0, 1, k, 1)
    relay(1)
    arrived(None, near_r[0], near_r[1])
    start(None, in_r[0])
    put_rhs(0, 1, 2, n_r[rows[0], 1])
    put_rhs(0, 2, 2, n_r[rows[1], tx(0)])

    arrived(has_far, f_mask)
    start(has_far, in_m[1])
    start(both(has_far, has_outer), out_m[1])
    for row in (0, 1):
        widen(6 + row, f_m[row])
    arrived(has_far, far_direct[0], far_direct[1])
    start(has_far, in_r[1])
    put_rhs(0, 1, 0, f_r[rows[0], 1])
    put_rhs(0, 2, 0, f_r[rows[1], tx(0)])
    arrived(has_far, far_direct[2])
    start(has_far, in_c[1][1])
    arrived(has_far, far_direct[5])
    start(both(has_far, has_outer), out_mid[1][1])
    for t, ks in ((0, (0, 1, 2)), (1, (0, 1))):
        for k in ks:
            put_column(0, f_c1, t, k, 2)
    arrived(has_far, far_c0[0], far_c0[1])
    start(has_far, in_c[1][0])
    start(both(has_far, has_outer), out_mid[1][0])
    for t, ks in ((0, (0, 1, 2)), (1, (0, 1))):
        for k in ks:
            put_column(0, f_c0, t, k, 1)

    arrived(has_outer, *direct_out)
    widen(3, g_m[1])
    for k, slot in ((1, core), (0, 1 - core)):
        for j in range(3):
            put(3, 1, k, j, g_c[1, slot, ty(j)], 3)
    put_rhs(1, 2, 1, g_r[1])

    near_c1[0].wait_recv()
    start(None, in_c[0][1])
    near_c1[1].wait_recv()
    start(has_outer, out_mid[0][1])
    for t, ks in ((0, (0, 1, 2)), (1, (0, 1))):
        for k in ks:
            put_column(2, n_c1, t, k, 0)

    def put_corner(x, side, ways):
        s = 2 - 2 * side
        for way in ways:
            for k, slot in (((1, 1 - core), (2, core)), ((1, core), (0, 1 - core)))[x]:
                put(3 * x, s, k, 1 if way == 0 else 2 * side, d_c[x, side, way, slot],
                    8 + 2 * x + side)

    for side in (1, 0):
        arrived(side_there[side], in_m[side], in_r[side], *in_c[side])
        widen(8 + side, d_m[0, side])
        put_corner(0, side, (0, 1))
        put_rhs(0, 0, 2 - 2 * side, d_r[0, side])

    def fold(value):
        return jnp.sum(value.reshape(-1, 8, b), axis=0)

    def column(value):
        return jnp.sum(value, axis=0, keepdims=True)

    def at_of(u, s):
        return slice(b * (3 * u + s), b * (3 * u + s) + b)

    members = [(u, s) for s in (1, 0, 2) for u in range(3)]

    def apply_row(solve, turn, u, s):
        found = near_three(s)
        strips = near_three(u)
        left = b * len(found) * (strips[0] + solve - first_row[u + solve])
        width = b * len(found) * len(strips)
        right = [vec[solve, turn, b * (3 * k + found[0]):b * (3 * k + found[0] + len(found)), :]
                 for k in strips]
        value = product(c_refs[u + solve][s, :, left:left + width], jnp.concatenate(right, axis=0))
        return value[0:b, 0:b] + (value[0:b, b:2 * b] + value[b:2 * b, 0:b])

    def solve_cluster(solve, between):
        gram = {}

        def power(j):
            sums = [jnp.zeros((8, b), F32) for _ in range(j + 1)]
            for u, s in members:
                value = apply_row(solve, (j - 1) % 2, u, s)
                basis[solve, j, at_of(u, s), :] = value
                for part, piece in enumerate(split(value)):
                    vec[solve, j % 2, at_of(u, s), b * part:b * part + b] = piece
                for i in range(j):
                    sums[i] = sums[i] + fold(value * basis[solve, i, at_of(u, s), :])
                sums[j] = sums[j] + fold(value * value)
            for i in range(j + 1):
                gram[i, j] = gram[j, i] = column(sums[i])
            between(j)

        def inner(left, other):
            result = None
            for i, a in enumerate(left):
                for k, c in enumerate(other):
                    term = (a * c) * gram[i, k]
                    result = term if result is None else result + term
            return result

        def norm_of(value):
            result = None
            for i, a in enumerate(value):
                for k in range(i, len(value)):
                    term = (a * value[k]) * gram[i, k] * (1.0 if i == k else 2.0)
                    result = term if result is None else result + term
            return jnp.maximum(result, 0.0)

        first_sums = jnp.zeros((8, b), F32)
        for u, s in members:
            value = basis[solve, 0, at_of(u, s), :]
            first_sums = first_sums + fold(value * value)
        gram[0, 0] = column(first_sums)
        counts = limits[rows[solve]].astype(F32)
        atom_of = (lax.broadcasted_iota(jnp.int32, (atoms, b), 1) // orb
                   == lax.broadcasted_iota(jnp.int32, (atoms, b), 0)).astype(F32)
        limit = product(jnp.broadcast_to(counts, (atoms, atoms)), atom_of)[0:1]

        power(1)
        norm = gram[0, 0]
        shadow = [jnp.ones_like(norm)]
        resid = y_first = shadow
        rho, floor = norm, 0.1 * norm
        tau = jnp.sqrt(norm)
        theta = eta = jnp.zeros_like(norm)
        u_first = along = image(y_first)
        direc, sol = [], []
        for n in range(1, ITERS + 1):
            active = (limit >= float(n)).astype(F32)
            if n > 1:
                power(2 * n - 1)
                rho_next = inner(shadow, resid)
                beta = guarded(rho_next, rho, floor)
                floor = 0.1 * jnp.sqrt(norm * size)
                rho = rho_next
                y_first = add(resid, beta, y_second)
                u_first = image(y_first)
                along = add(u_first, beta, add(u_second, beta, along))
            alpha = guarded(
                rho, inner(shadow, along), 0.1 * jnp.sqrt(norm * (norm_of(along) + 1e-06)))
            ratio = guarded(1.0, alpha, 0.1)
            y_second = add(y_first, -alpha, along)
            u_second = image(y_second)
            for part, (y, u_of) in enumerate(((y_first, u_first), (y_second, u_second))):
                resid = add(resid, -alpha, u_of)
                direc = add(y, theta * theta * eta * ratio, direc)
                if part == 1 and n == ITERS:
                    sums = jnp.zeros((8, b), F32)
                    for u, s in members:
                        value = apply_row(solve, (2 * n - 1) % 2, u, s) * resid[2 * n]
                        for i in range(2 * n):
                            value = value + basis[solve, i, at_of(u, s), :] * resid[i]
                        sums = sums + fold(value * value)
                    size = column(sums)
                else:
                    if part == 1:
                        power(2 * n)
                    size = norm_of(resid)
                theta = jnp.sqrt(size) / tau
                cosine = 1.0 / jnp.sqrt(1.0 + theta * theta)
                tau = tau * theta * cosine
                eta = cosine * cosine * alpha
                sol = add(sol, active * eta, direc)

        for u, s in members:
            value = basis[solve, 0, at_of(u, s), :] * sol[0]
            for i in range(1, 2 * ITERS):
                value = value + basis[solve, i, at_of(u, s), :] * sol[i]
            out[rows[solve], 3 * tx(u) + ty(s)] = value

    def between(j):
        if j == 1:
            relay(2)
            near_c0[2].wait_recv()
            start(has_hop, far_c0[2])
            start(has_outer, out_end[0][0])
            near_c1[2].wait_recv()
            start(has_outer, out_end[0][1])
            put_column(2, n_c0, 1, 2, 1)
            put_column(2, n_c1, 1, 2, 0)
        if j == 2:
            arrived(has_far, far_direct[6])
            start(both(has_far, has_outer), out_end[1][1])
            put_column(0, f_c1, 1, 2, 2)
            arrived(has_outer, out_m[0], *out_mid[0])
            arrived(both(has_far, has_outer), out_m[1], *out_mid[1])
            for side in (0, 1):
                widen(10 + side, d_m[1, side])
        if j == 3:
            arrived(has_far, far_c0[2])
            start(both(has_far, has_outer), out_end[1][0])
            put_column(0, f_c0, 1, 2, 1)
            near_r[2].wait_recv()
            start(has_outer, out_r[0])
            put_rhs(1, 1, 2, n_r[rows[1], 1])
        if j == 4:
            arrived(has_far, far_direct[3])
            start(both(has_far, has_outer), out_r[1])
            put_rhs(1, 1, 0, f_r[rows[1], 1])
            arrived(has_far, far_direct[4])
            put_rhs(1, 0, 0, f_r[rows[0], tx(2)])
        if j == 5:
            near_r[3].wait_recv()
            put_rhs(1, 0, 2, n_r[rows[0], tx(2)])
            arrived(has_outer, out_r[0], *out_end[0])
            arrived(both(has_far, has_outer), out_r[1], *out_end[1])
            for side in (0, 1):
                put_corner(1, side, (0, 1))
                put_rhs(1, 2, 2 - 2 * side, d_r[1, side])

    solve_cluster(0, between)
    solve_cluster(1, lambda j: None)

    sent(None, n_mask, *near_c0, *near_c1, *near_r, *direct_in, in_m[0], in_r[0], *in_c[0])
    sent(has_hop, f_mask, *far_c0)
    for i, copy in enumerate(far_direct):
        sent(both(has_far, jnp.logical_not(is_relayed(i))), copy)
    for i, copy in enumerate(far_pass):
        sent(is_relayed(i), copy)
        sent(far_group[i] < partner_relayed, far_hop[i])
    sent(has_outer, *direct_out)
    for side in (0, 1):
        if side:
            sent(has_far, in_m[1], in_r[1], *in_c[1])
        sent(has_outer if side == 0 else both(has_far, has_outer),
             out_m[side], out_r[side], *out_mid[side], *out_end[side])
    assert all(sum(1 for key in numbers if key[0] == kind) <= COPIES for kind in ("send", "recv"))


def shards(blocks, pair_mask, rhs_rows, counts):
    groups = blocks.shape[0]
    b = blocks.shape[-1]
    atoms = pair_mask.shape[-1]
    offsets = pair_mask.shape[2]
    blocks = blocks.reshape(groups, 3, 3, b, b)
    rhs = rhs_rows.reshape(groups, 3, 3, b, b)
    masks = pair_mask.transpose(0, 1, 3, 4, 2).reshape(groups, atoms, atoms, offsets)
    any_spec = pl.BlockSpec(memory_space=pl.ANY)
    vmem_spec = pl.BlockSpec(memory_space=pltpu.VMEM)

    def raw(*lead):
        return pltpu.VMEM(lead + (b, b), F32)

    def flags(*lead):
        return pltpu.VMEM(lead + (atoms, atoms, offsets), jnp.int32)

    solved = pl.pallas_call(
        kernel,
        out_shape=pltpu.VMEM((groups, 9, b, b), F32),
        in_specs=[any_spec, any_spec, any_spec, vmem_spec, vmem_spec],
        out_specs=vmem_spec,
        scratch_shapes=[
            raw(groups, 3, 3), raw(2, 2, 3), raw(groups, 3), raw(groups, 3), raw(groups, 3),
            raw(groups, 3), raw(2, 2, 2, 2), raw(9),
            raw(4), raw(2), raw(groups, 3), raw(groups, 3), raw(2, 2),
            flags(groups), flags(groups), flags(2), flags(2, 2),
            pltpu.VMEM((12, offsets, atoms * b), F32),
            pltpu.VMEM((3, 2 * b, 6 * b), BF16),
            pltpu.VMEM((3, 2 * b, 9 * b), BF16),
            pltpu.VMEM((3, 2 * b, 9 * b), BF16),
            pltpu.VMEM((3, 2 * b, 6 * b), BF16),
            pltpu.VMEM((2, 2, 9 * b, 2 * b), BF16),
            pltpu.VMEM((2, 2 * ITERS, 9 * b, b), F32),
            pltpu.SemaphoreType.DMA((COPIES,)),
            pltpu.SemaphoreType.DMA((COPIES,)),
            pltpu.SemaphoreType.DMA((5,)),
        ],
        compiler_params=pltpu.CompilerParams(
            collective_id=0, has_side_effects=True, vmem_limit_bytes=60 * 1024 * 1024
        ),
    )(blocks, masks, rhs, counts, masks)
    return solved.reshape(groups, 1, 9, b, b)


def solution(mesh):
    spec = P("gx", "gy", None, None, None)
    return jax.shard_map(
        shards,
        mesh=mesh,
        in_specs=(spec, spec, spec, P("gx", "gy", None)),
        out_specs=spec,
        check_vma=False,
    )
```

```python
import jax
import jax.numpy as jnp
from jax import lax
from jax.experimental import pallas as pl
from jax.experimental.pallas import tpu as pltpu
from jax.sharding import PartitionSpec as P

ITERS = 3
COPIES = 80
MESH = pl.DeviceIdType.MESH
F32 = jnp.float32
BF16 = jnp.bfloat16


def guarded(top, bottom, floor_val):
    return top * bottom / (bottom * bottom + floor_val * floor_val)


def split(value):
    high = value.astype(BF16)
    return high, (value - high.astype(F32)).astype(BF16)


def product(left, right):
    return jnp.dot(left, right, preferred_element_type=F32)


def near_three(s):
    return range(max(0, s - 1), min(3, s + 2))


def add(left, factor, right):
    result = []
    for k in range(max(len(left), len(right))):
        a = left[k] if k < len(left) else None
        c = right[k] if k < len(right) else None
        if c is None:
            result.append(a)
        else:
            result.append(factor * c if a is None else a + factor * c)
    return result


def image(value):
    return add(list(value) + [None], -1.0, [None] + list(value))


def kernel(
    blocks, masks, rhs, counts, out,
    own_c, g_c, n_c0, n_c1, f_c0, f_c1, d_c, passing,
    o_r, g_r, n_r, f_r, d_r, own_masks, n_m, f_m, g_m, d_m, limits, wide,
    c_of0, c_of1, c_of2, c_of3, vec, basis,
    send_sem, recv_sem, local_sem,
):
    b = blocks.shape[-1]
    atoms = masks.shape[1]
    offsets = masks.shape[-1]
    orb = b // atoms
    gx, gy = lax.axis_index("gx"), lax.axis_index("gy")
    ngx, ngy = lax.axis_size("gx"), lax.axis_size("gy")
    assert ngx % 2 == 0 and ngy % 2 == 0
    half = ngy // 2
    core, odd = gx % 2, gy % 2
    step_x, step_y = 1 - 2 * core, 1 - 2 * odd
    inner_dev, outer_dev = (gx + step_x, gy), (gx - step_x, gy)
    near_dev, far_dev, hop_dev = (gx, gy + step_y), (gx, gy - step_y), (gx, gy + 2 * step_y)

    def inside(index, size):
        return jnp.logical_and(index >= 0, index < size)

    both = jnp.logical_and
    has_outer = inside(gx - step_x, ngx)
    has_far = inside(gy - step_y, ngy)
    has_hop = inside(gy + 2 * step_y, ngy)
    side_there = (None, has_far)
    rank = jnp.where(odd == 0, gy // 2, half - 1 - gy // 2)
    mine_relayed = (4 * rank) // half
    partner_relayed = (4 * (half - 1 - rank)) // half

    def ty(j):
        return 1 if j == 1 else 2 * odd + step_y * j

    def tx(k):
        return 1 if k == 1 else 2 * (1 - core) - step_x * k

    rows = (1 - core, core)
    head, tail = pl.ds(1 - core, 2), pl.ds(core, 2)
    full = pl.ds(0, 3)

    numbers = {}

    def number(kind, name):
        return numbers.setdefault((kind, name), sum(1 for key in numbers if key[0] == kind))

    def remote(src, dst, device, name, arrival=None):
        return pltpu.make_async_remote_copy(
            src_ref=src, dst_ref=dst, send_sem=send_sem.at[number("send", name)],
            recv_sem=recv_sem.at[number("recv", arrival or name)],
            device_id=device, device_id_type=MESH,
        )

    n_mask = remote(masks, n_m, near_dev, "nm")
    f_mask = remote(n_m, f_m, hop_dev, "fm")
    far_parts = (
        (0, rhs, f_r, rows[0], head, (0, 2)), (0, rhs, f_r, rows[1], pl.ds(tx(0), 1), (2, 1)),
        (1, blocks, f_c1, rows[0], full, (3, 3)),
        (2, rhs, f_r, rows[1], tail, (6, 2)), (2, rhs, f_r, rows[0], pl.ds(tx(2), 1), (8, 1)),
        (4, blocks, f_c1, rows[1], head, None), (4, blocks, f_c1, rows[1], pl.ds(tx(2), 1), None),
    )
    far_direct, far_pass, far_hop, far_group = [], [], [], []
    for i, (group, source, target, row, ous, slot) in enumerate(far_parts):
        src, dst = source.at[row, ous, ty(0)], target.at[row, ous]
        far_group.append(group)
        far_direct.append(remote(src, dst, far_dev, ("fd", i), ("fg", i)))
        if slot is not None:
            held = passing.at[pl.ds(*slot)]
            far_pass.append(remote(src, held, near_dev, ("fp", i)))
            far_hop.append(remote(held, dst, hop_dev, ("fh", i), ("fg", i)))

    c_parts = ((rows[0], full), (rows[1], head), (rows[1], pl.ds(tx(2), 1)))
    near_c0 = [remote(blocks.at[row, ous, 1], n_c0.at[row, ous], near_dev, ("n0", i))
               for i, (row, ous) in enumerate(c_parts)]
    near_c1 = [remote(blocks.at[row, ous, ty(2)], n_c1.at[row, ous], near_dev, ("n1", i))
               for i, (row, ous) in enumerate(c_parts)]
    far_c0 = [remote(n_c0.at[row, ous], f_c0.at[row, ous], hop_dev, ("f0", i))
              for i, (row, ous) in enumerate(c_parts)]
    near_r = [remote(rhs.at[row, ous, ty(2)], n_r.at[row, ous], near_dev, ("nr", i))
              for i, (row, ous) in enumerate((
                  (rows[0], head), (rows[1], pl.ds(tx(0), 1)), (rows[1], pl.ds(tx(2), 1)),
                  (rows[1], pl.ds(1, 1)), (rows[0], pl.ds(tx(2), 1))))]

    direct_in = [
        remote(masks.at[rows[0]], g_m.at[0], inner_dev, "gm0"),
        remote(rhs.at[rows[0], tx(0), 1], g_r.at[0], inner_dev, "gr0"),
        remote(blocks.at[rows[0], head], g_c.at[0], inner_dev, "gc0"),
    ]
    direct_out = [
        remote(masks.at[rows[1]], g_m.at[1], outer_dev, "gm1"),
        remote(rhs.at[rows[1], tx(2), 1], g_r.at[1], outer_dev, "gr1"),
        remote(blocks.at[rows[1], tail], g_c.at[1], outer_dev, "gc1"),
    ]
    in_m, in_r, in_c, out_m, out_r, out_mid, out_end = [], [], [], [], [], [], []
    for side, (m, r, coupled) in enumerate(((n_m, n_r, (n_c0, n_c1)), (f_m, f_r, (f_c0, f_c1)))):
        in_m.append(remote(m.at[rows[0]], d_m.at[0, side], inner_dev, ("im", side)))
        in_r.append(remote(r.at[rows[0], tx(0)], d_r.at[0, side], inner_dev, ("ir", side)))
        out_m.append(remote(m.at[rows[1]], d_m.at[1, side], outer_dev, ("om", side)))
        out_r.append(remote(r.at[rows[1], tx(2)], d_r.at[1, side], outer_dev, ("or", side)))
        in_c.append([remote(c.at[rows[0], head], d_c.at[0, side, k], inner_dev, ("ic", side, k))
                     for k, c in enumerate(coupled)])
        out_mid.append([remote(c.at[rows[1], 1], d_c.at[1, side, k, 1 - core], outer_dev, ("oc", side, k))
                        for k, c in enumerate(coupled)])
        out_end.append([remote(c.at[rows[1], tx(2)], d_c.at[1, side, k, core], outer_dev, ("oe", side, k))
                        for k, c in enumerate(coupled)])

    barrier = pltpu.get_barrier_semaphore()
    total = jnp.int32(0)
    peers = [(inside(gx + step, ngx), (gx + step, gy)) for step in (-1, 1)]
    peers += [(inside(gy + step, ngy), (gx, gy + step)) for step in (-2, -1, 1, 2)]
    for exists, device in peers:
        total = total + exists.astype(jnp.int32)

        @pl.when(exists)
        def _(device=device):
            pl.semaphore_signal(barrier, inc=1, device_id=device, device_id_type=MESH)
    pl.semaphore_wait(barrier, total)

    def on(condition, actions):
        if condition is None:
            for action in actions:
                action()
        else:
            @pl.when(condition)
            def _():
                for action in actions:
                    action()

    def start(condition, *copies):
        on(condition, [copy.start for copy in copies])

    def arrived(condition, *copies):
        on(condition, [copy.wait_recv for copy in copies])

    def sent(condition, *copies):
        on(condition, [copy.wait_send for copy in copies])

    def is_relayed(i):
        return far_group[i] < mine_relayed

    def start_pass(group):
        for i, copy in enumerate(far_pass):
            if far_group[i] == group:
                start(is_relayed(i), copy)

    def start_direct(i):
        start(both(has_far, jnp.logical_not(is_relayed(i))), far_direct[i])

    def relay(group):
        for i, copy in enumerate(far_pass):
            if far_group[i] == group:
                @pl.when(group < partner_relayed)
                def _(i=i, copy=copy):
                    copy.wait_recv()
                    far_hop[i].start()

    n_mask.start()
    start_pass(0)
    start(None, near_c0[0], near_c0[1])
    start_pass(1)
    start(None, near_r[0], near_r[1], near_c1[0], near_c1[1])
    for i in (0, 1, 2, 5):
        start_direct(i)
    start(None, *direct_in)
    start(has_outer, *direct_out)
    start_pass(2)
    start(None, near_c0[2], near_r[2], near_c1[2], near_r[3], near_r[4])
    for i in (6, 3, 4):
        start_direct(i)

    local_c = pltpu.make_async_copy(blocks, own_c, local_sem.at[0])
    own_rhs = ((0, 1, 0, 1), (0, 2, 1, 0), (1, 0, 0, 2), (1, 1, 1, 1))
    local_r = [pltpu.make_async_copy(rhs.at[rows[t], tx(k), 1], o_r.at[i], local_sem.at[1 + i])
               for i, (_, _, t, k) in enumerate(own_rhs)]
    local_m = pltpu.make_async_copy(masks, own_masks, local_sem.at[5])
    local_n = pltpu.make_async_copy(counts, limits, local_sem.at[6])
    start(None, local_m, local_c, local_n, *local_r)

    def clear(*refs):
        for ref in refs:
            ref[...] = jnp.zeros(ref.shape, ref.dtype)

    @pl.when(jnp.logical_not(has_far))
    def _():
        clear(f_c0, f_c1, f_r, f_m, *[d.at[x, 1] for d in (d_c, d_r, d_m) for x in (0, 1)])

    @pl.when(jnp.logical_not(has_outer))
    def _():
        clear(g_c.at[1], g_r.at[1], g_m.at[1], d_c.at[1], d_r.at[1], d_m.at[1])

    wide_shape = (atoms * atoms, atoms * b)
    above, across = (lax.broadcasted_iota(jnp.int32, wide_shape, d) for d in (0, 1))
    spread = (above == atoms * (across // b) + across % b // orb).astype(F32)

    def widen(index, value):
        flat = value.astype(F32).reshape(atoms * atoms, offsets)
        wide[index] = lax.dot_general(
            flat, spread, (((0,), (0,)), ((), ())), preferred_element_type=F32)

    c_refs = (c_of0, c_of1, c_of2, c_of3)
    first_row = (0, 0, 1, 2)

    def put(w, s, k, j, value, mask):
        mask_row = wide[mask, pl.ds(3 * tx(k) + ty(j), 1), :]
        found = near_three(s)
        col = b * ((w + k - 1 - first_row[w]) * len(found) + s + j - 1 - found[0])
        for i in range(atoms):
            masked = value[orb * i:orb * (i + 1)] * mask_row[:, b * i:b * (i + 1)]
            for part, piece in enumerate(split(masked)):
                at = b * part + orb * i
                c_refs[w][s, at:at + orb, col:col + b] = piece

    def put_rhs(solve, u, s, value):
        at = b * (3 * u + s)
        basis[solve, 0, at:at + b, :] = value
        for part, piece in enumerate(split(value)):
            vec[solve, 0, at:at + b, b * part:b * part + b] = piece

    local_m.wait()
    for row in (0, 1):
        widen(row, own_masks[row])
    local_c.wait()
    local_n.wait()
    for t in (0, 1):
        for k in range(3):
            for j in range(3):
                put(1 + t, 1, k, j, own_c[rows[t], tx(k), ty(j)], rows[t])
    for i, (solve, u, _, _) in enumerate(own_rhs):
        local_r[i].wait()
        put_rhs(solve, u, 1, o_r[i])

    arrived(None, *direct_in)
    widen(2, g_m[0])
    for k, slot in ((1, 1 - core), (2, core)):
        for j in range(3):
            put(0, 1, k, j, g_c[0, slot, ty(j)], 2)
    put_rhs(0, 0, 1, g_r[0])

    n_mask.wait_recv()
    start(has_hop, f_mask)
    start(None, in_m[0])
    start(has_outer, out_m[0])
    relay(0)
    for row in (0, 1):
        widen(4 + row, n_m[row])

    def put_column(s, ref, t, k, j):
        put(1 + t, s, k, j, ref[rows[t], tx(k)], (4 if s == 2 else 6) + rows[t])

    near_c0[0].wait_recv()
    start(has_hop, far_c0[0])
    start(None, in_c[0][0])
    for k in range(3):
        put_column(2, n_c0, 0, k, 1)
    near_c0[1].wait_recv()
    start(has_hop, far_c0[1])
    start(has_outer, out_mid[0][0])
    for k in (0, 1):
        put_column(2, n_c0, 1, k, 1)
    relay(1)
    arrived(None, near_r[0], near_r[1])
    start(None, in_r[0])
    put_rhs(0, 1, 2, n_r[rows[0], 1])
    put_rhs(0, 2, 2, n_r[rows[1], tx(0)])

    arrived(has_far, f_mask)
    start(has_far, in_m[1])
    start(both(has_far, has_outer), out_m[1])
    for row in (0, 1):
        widen(6 + row, f_m[row])
    arrived(has_far, far_direct[0], far_direct[1])
    start(has_far, in_r[1])
    put_rhs(0, 1, 0, f_r[rows[0], 1])
    put_rhs(0, 2, 0, f_r[rows[1], tx(0)])
    arrived(has_far, far_direct[2])
    start(has_far, in_c[1][1])
    arrived(has_far, far_direct[5])
    start(both(has_far, has_outer), out_mid[1][1])
    for t, ks in ((0, (0, 1, 2)), (1, (0, 1))):
        for k in ks:
            put_column(0, f_c1, t, k, 2)
    arrived(has_far, far_c0[0], far_c0[1])
    start(has_far, in_c[1][0])
    start(both(has_far, has_outer), out_mid[1][0])
    for t, ks in ((0, (0, 1, 2)), (1, (0, 1))):
        for k in ks:
            put_column(0, f_c0, t, k, 1)

    arrived(has_outer, *direct_out)
    widen(3, g_m[1])
    for k, slot in ((1, core), (0, 1 - core)):
        for j in range(3):
            put(3, 1, k, j, g_c[1, slot, ty(j)], 3)
    put_rhs(1, 2, 1, g_r[1])

    near_c1[0].wait_recv()
    start(None, in_c[0][1])
    near_c1[1].wait_recv()
    start(has_outer, out_mid[0][1])
    for t, ks in ((0, (0, 1, 2)), (1, (0, 1))):
        for k in ks:
            put_column(2, n_c1, t, k, 0)

    def put_corner(x, side, ways):
        s = 2 - 2 * side
        for way in ways:
            for k, slot in (((1, 1 - core), (2, core)), ((1, core), (0, 1 - core)))[x]:
                put(3 * x, s, k, 1 if way == 0 else 2 * side, d_c[x, side, way, slot],
                    8 + 2 * x + side)

    for side in (1, 0):
        arrived(side_there[side], in_m[side], in_r[side], *in_c[side])
        widen(8 + side, d_m[0, side])
        put_corner(0, side, (0, 1))
        put_rhs(0, 0, 2 - 2 * side, d_r[0, side])

    def fold(value):
        return jnp.sum(value.reshape(-1, 8, b), axis=0)

    def column(value):
        return jnp.sum(value, axis=0, keepdims=True)

    def at_of(u, s):
        return slice(b * (3 * u + s), b * (3 * u + s) + b)

    members = [(u, s) for s in (1, 0, 2) for u in range(3)]

    def apply_row(solve, turn, u, s, only=(0, 1, 2), low=True):
        found = near_three(s)
        used = [k for k in found if k in only]
        if not used:
            return None
        strips = near_three(u)
        ref, first = c_refs[u + solve], strips[0] + solve - first_row[u + solve]
        height = slice(0, 2 * b if low else b)
        if len(used) == len(found):
            left = ref[s, height, b * len(found) * first:b * len(found) * (first + len(strips))]
        else:
            starts = [b * (len(found) * (first + i) + used[0] - found[0]) for i in range(len(strips))]
            left = jnp.concatenate(
                [ref[s, height, at:at + b * len(used)] for at in starts], axis=1)
        right = [vec[solve, turn, b * (3 * k + used[0]):b * (3 * k + used[0] + len(used)), :]
                 for k in strips]
        value = product(left, jnp.concatenate(right, axis=0))
        total = value[0:b, 0:b] + value[0:b, b:2 * b]
        return total + value[b:2 * b, 0:b] if low else total

    def before_near(u, s):
        return () if (u, s) == (2, 2) else (0, 1, 2) if s == 0 else (0, 1)

    def first_product(solve):
        for u, s in members:
            value = apply_row(solve, 0, u, s, before_near(u, s))
            if value is not None:
                basis[solve, 1, at_of(u, s), :] = value

    def rest_of_first(solve, u, s):
        done = before_near(u, s)
        value = apply_row(solve, 0, u, s, tuple(k for k in range(3) if k not in done))
        if not done:
            return value
        partial = basis[solve, 1, at_of(u, s), :]
        return partial if value is None else partial + value

    def solve_cluster(solve, between):
        gram = {}

        def power(j):
            sums = [jnp.zeros((8, b), F32) for _ in range(j + 1)]
            for u, s in members:
                if j == 1 and solve == 1:
                    value = rest_of_first(solve, u, s)
                else:
                    value = apply_row(solve, (j - 1) % 2, u, s)
                basis[solve, j, at_of(u, s), :] = value
                for part, piece in enumerate(split(value)):
                    vec[solve, j % 2, at_of(u, s), b * part:b * part + b] = piece
                for i in range(j):
                    sums[i] = sums[i] + fold(value * basis[solve, i, at_of(u, s), :])
                sums[j] = sums[j] + fold(value * value)
            for i in range(j + 1):
                gram[i, j] = gram[j, i] = column(sums[i])
            between(j)

        def inner(left, other):
            result = None
            for i, a in enumerate(left):
                for k, c in enumerate(other):
                    term = (a * c) * gram[i, k]
                    result = term if result is None else result + term
            return result

        def norm_of(value):
            result = None
            for i, a in enumerate(value):
                for k in range(i, len(value)):
                    term = (a * value[k]) * gram[i, k] * (1.0 if i == k else 2.0)
                    result = term if result is None else result + term
            return jnp.maximum(result, 0.0)

        first_sums = jnp.zeros((8, b), F32)
        for u, s in members:
            value = basis[solve, 0, at_of(u, s), :]
            first_sums = first_sums + fold(value * value)
        gram[0, 0] = column(first_sums)
        count = limits[rows[solve]].astype(F32)
        atom_of = (lax.broadcasted_iota(jnp.int32, (atoms, b), 1) // orb
                   == lax.broadcasted_iota(jnp.int32, (atoms, b), 0)).astype(F32)
        limit = product(jnp.broadcast_to(count, (atoms, atoms)), atom_of)[0:1]

        power(1)
        norm = gram[0, 0]
        shadow = [jnp.ones_like(norm)]
        resid = y_first = shadow
        rho, floor = norm, 0.1 * norm
        tau = jnp.sqrt(norm)
        theta = eta = jnp.zeros_like(norm)
        u_first = along = image(y_first)
        direc, sol = [], []
        for n in range(1, ITERS + 1):
            active = (limit >= float(n)).astype(F32)
            if n > 1:
                power(2 * n - 1)
                rho_next = inner(shadow, resid)
                beta = guarded(rho_next, rho, floor)
                floor = 0.1 * jnp.sqrt(norm * size)
                rho = rho_next
                y_first = add(resid, beta, y_second)
                u_first = image(y_first)
                along = add(u_first, beta, add(u_second, beta, along))
            alpha = guarded(
                rho, inner(shadow, along), 0.1 * jnp.sqrt(norm * (norm_of(along) + 1e-06)))
            ratio = guarded(1.0, alpha, 0.1)
            y_second = add(y_first, -alpha, along)
            u_second = image(y_second)
            for part, (y, u_of) in enumerate(((y_first, u_first), (y_second, u_second))):
                resid = add(resid, -alpha, u_of)
                direc = add(y, theta * theta * eta * ratio, direc)
                if part == 1 and n == ITERS:
                    sums = jnp.zeros((8, b), F32)
                    for u, s in members:
                        value = apply_row(solve, (2 * n - 1) % 2, u, s, low=False)
                        value = value * resid[2 * n]
                        for i in range(2 * n):
                            value = value + basis[solve, i, at_of(u, s), :] * resid[i]
                        sums = sums + fold(value * value)
                    size = column(sums)
                else:
                    if part == 1:
                        power(2 * n)
                    size = norm_of(resid)
                theta = jnp.sqrt(size) / tau
                cosine = 1.0 / jnp.sqrt(1.0 + theta * theta)
                tau = tau * theta * cosine
                eta = cosine * cosine * alpha
                sol = add(sol, active * eta, direc)

        for u, s in members:
            value = basis[solve, 0, at_of(u, s), :] * sol[0]
            for i in range(1, 2 * ITERS):
                value = value + basis[solve, i, at_of(u, s), :] * sol[i]
            out[rows[solve], 3 * tx(u) + ty(s)] = value

    def between(j):
        if j == 1:
            relay(2)
            near_c0[2].wait_recv()
            start(has_hop, far_c0[2])
            start(has_outer, out_end[0][0])
            put_column(2, n_c0, 1, 2, 1)
        if j == 2:
            arrived(has_outer, out_m[0], *out_mid[0])
            arrived(both(has_far, has_outer), out_m[1], *out_mid[1])
            for side in (0, 1):
                widen(10 + side, d_m[1, side])
            near_r[2].wait_recv()
            start(has_outer, out_r[0])
        if j == 3:
            arrived(has_far, far_direct[6])
            start(both(has_far, has_outer), out_end[1][1])
            put_column(0, f_c1, 1, 2, 2)
        if j == 4:
            near_c1[2].wait_recv()
            start(has_outer, out_end[0][1])
            put_column(2, n_c1, 1, 2, 0)
            arrived(has_far, far_direct[3])
            start(both(has_far, has_outer), out_r[1])
            put_rhs(1, 1, 0, f_r[rows[1], 1])
        if j == 5:
            arrived(has_far, far_c0[2], far_direct[4])
            start(both(has_far, has_outer), out_end[1][0])
            put_column(0, f_c0, 1, 2, 1)
            put_rhs(1, 0, 0, f_r[rows[0], tx(2)])

    solve_cluster(0, between)
    arrived(both(has_far, has_outer), out_r[1], *out_end[1])
    put_corner(1, 1, (0, 1))
    put_rhs(1, 2, 0, d_r[1, 1])
    first_product(1)
    arrived(has_outer, out_r[0], *out_end[0])
    put_corner(1, 0, (0, 1))
    put_rhs(1, 2, 2, d_r[1, 0])
    arrived(None, near_r[3], near_r[4])
    put_rhs(1, 1, 2, n_r[rows[1], 1])
    put_rhs(1, 0, 2, n_r[rows[0], tx(2)])
    solve_cluster(1, lambda j: None)

    sent(None, n_mask, *near_c0, *near_c1, *near_r, *direct_in, in_m[0], in_r[0], *in_c[0])
    sent(has_hop, f_mask, *far_c0)
    for i, copy in enumerate(far_direct):
        sent(both(has_far, jnp.logical_not(is_relayed(i))), copy)
    for i, copy in enumerate(far_pass):
        sent(is_relayed(i), copy)
        sent(far_group[i] < partner_relayed, far_hop[i])
    sent(has_outer, *direct_out)
    for side in (0, 1):
        if side:
            sent(has_far, in_m[1], in_r[1], *in_c[1])
        sent(has_outer if side == 0 else both(has_far, has_outer),
             out_m[side], out_r[side], *out_mid[side], *out_end[side])
    assert all(sum(1 for key in numbers if key[0] == kind) <= COPIES for kind in ("send", "recv"))


def shards(blocks, pair_mask, rhs_rows, counts):
    groups = blocks.shape[0]
    b = blocks.shape[-1]
    atoms = pair_mask.shape[-1]
    offsets = pair_mask.shape[2]
    blocks = blocks.reshape(groups, 3, 3, b, b)
    rhs = rhs_rows.reshape(groups, 3, 3, b, b)
    masks = pair_mask.transpose(0, 1, 3, 4, 2).reshape(groups, atoms, atoms, offsets)
    any_spec = pl.BlockSpec(memory_space=pl.ANY)
    vmem_spec = pl.BlockSpec(memory_space=pltpu.VMEM)

    def raw(*lead):
        return pltpu.VMEM(lead + (b, b), F32)

    def flags(*lead):
        return pltpu.VMEM(lead + (atoms, atoms, offsets), jnp.int32)

    solved = pl.pallas_call(
        kernel,
        out_shape=pltpu.VMEM((groups, 9, b, b), F32),
        in_specs=[any_spec, any_spec, any_spec, any_spec],
        out_specs=vmem_spec,
        scratch_shapes=[
            raw(groups, 3, 3), raw(2, 2, 3), raw(groups, 3), raw(groups, 3), raw(groups, 3),
            raw(groups, 3), raw(2, 2, 2, 2), raw(9),
            raw(4), raw(2), raw(groups, 3), raw(groups, 3), raw(2, 2),
            flags(groups), flags(groups), flags(groups), flags(2), flags(2, 2),
            pltpu.VMEM(counts.shape, jnp.int32),
            pltpu.VMEM((12, offsets, atoms * b), F32),
            pltpu.VMEM((3, 2 * b, 6 * b), BF16),
            pltpu.VMEM((3, 2 * b, 9 * b), BF16),
            pltpu.VMEM((3, 2 * b, 9 * b), BF16),
            pltpu.VMEM((3, 2 * b, 6 * b), BF16),
            pltpu.VMEM((2, 2, 9 * b, 2 * b), BF16),
            pltpu.VMEM((2, 2 * ITERS, 9 * b, b), F32),
            pltpu.SemaphoreType.DMA((COPIES,)),
            pltpu.SemaphoreType.DMA((COPIES,)),
            pltpu.SemaphoreType.DMA((7,)),
        ],
        compiler_params=pltpu.CompilerParams(
            collective_id=0, has_side_effects=True, vmem_limit_bytes=60 * 1024 * 1024
        ),
    )(blocks, masks, rhs, counts)
    return solved.reshape(groups, 1, 9, b, b)


def solution(mesh):
    spec = P("gx", "gy", None, None, None)
    return jax.shard_map(
        shards,
        mesh=mesh,
        in_specs=(spec, spec, spec, P("gx", "gy", None)),
        out_specs=spec,
        check_vma=False,
    )
```

```python
import jax
import jax.numpy as jnp
from jax import lax
from jax.experimental import pallas as pl
from jax.experimental.pallas import tpu as pltpu
from jax.sharding import PartitionSpec as P

ITERS = 3
COPIES = 80
MESH = pl.DeviceIdType.MESH
F32 = jnp.float32
BF16 = jnp.bfloat16


def guarded(top, bottom, floor_val):
    return top * bottom / (bottom * bottom + floor_val * floor_val)


def split(value):
    high = value.astype(BF16)
    return high, (value - high.astype(F32)).astype(BF16)


def product(left, right):
    return jnp.dot(left, right, preferred_element_type=F32)


def near_three(s):
    return range(max(0, s - 1), min(3, s + 2))


def add(left, factor, right):
    result = []
    for k in range(max(len(left), len(right))):
        a = left[k] if k < len(left) else None
        c = right[k] if k < len(right) else None
        if c is None:
            result.append(a)
        else:
            result.append(factor * c if a is None else a + factor * c)
    return result


def image(value):
    return add(list(value) + [None], -1.0, [None] + list(value))


def kernel(
    blocks, masks, rhs, counts, out,
    own_c, g_c, n_c0, n_c1, f_c0, f_c1, d_c, passing,
    o_r, g_r, n_r, f_r, d_r, own_masks, own_m, n_m, f_m, g_m, d_m, limits, wide,
    c_of0, c_of1, c_of2, c_of3, vec, basis,
    send_sem, recv_sem, local_sem,
):
    b = blocks.shape[-1]
    atoms = masks.shape[1]
    offsets = masks.shape[-1]
    orb = b // atoms
    gx, gy = lax.axis_index("gx"), lax.axis_index("gy")
    ngx, ngy = lax.axis_size("gx"), lax.axis_size("gy")
    assert ngx % 2 == 0 and ngy % 2 == 0
    half = ngy // 2
    core, odd = gx % 2, gy % 2
    step_x, step_y = 1 - 2 * core, 1 - 2 * odd
    inner_dev, outer_dev = (gx + step_x, gy), (gx - step_x, gy)
    near_dev, far_dev, hop_dev = (gx, gy + step_y), (gx, gy - step_y), (gx, gy + 2 * step_y)

    def inside(index, size):
        return jnp.logical_and(index >= 0, index < size)

    both = jnp.logical_and
    has_outer = inside(gx - step_x, ngx)
    has_far = inside(gy - step_y, ngy)
    has_hop = inside(gy + 2 * step_y, ngy)
    side_there = (None, has_far)
    rank = jnp.where(odd == 0, gy // 2, half - 1 - gy // 2)
    mine_relayed = (4 * rank) // half
    partner_relayed = (4 * (half - 1 - rank)) // half

    def ty(j):
        return 1 if j == 1 else 2 * odd + step_y * j

    def tx(k):
        return 1 if k == 1 else 2 * (1 - core) - step_x * k

    rows = (1 - core, core)
    head, tail = pl.ds(1 - core, 2), pl.ds(core, 2)
    full = pl.ds(0, 3)

    numbers = {}

    def number(kind, name):
        return numbers.setdefault((kind, name), sum(1 for key in numbers if key[0] == kind))

    def remote(src, dst, device, name, arrival=None):
        return pltpu.make_async_remote_copy(
            src_ref=src, dst_ref=dst, send_sem=send_sem.at[number("send", name)],
            recv_sem=recv_sem.at[number("recv", arrival or name)],
            device_id=device, device_id_type=MESH,
        )

    n_mask = remote(own_m, n_m, near_dev, "nm")
    f_mask = remote(n_m, f_m, hop_dev, "fm")
    far_parts = (
        (0, rhs, f_r, rows[0], head, (0, 2)), (0, rhs, f_r, rows[1], pl.ds(tx(0), 1), (2, 1)),
        (1, blocks, f_c1, rows[0], full, (3, 3)),
        (2, rhs, f_r, rows[1], tail, (6, 2)), (2, rhs, f_r, rows[0], pl.ds(tx(2), 1), (8, 1)),
        (4, blocks, f_c1, rows[1], head, None), (4, blocks, f_c1, rows[1], pl.ds(tx(2), 1), None),
    )
    far_direct, far_pass, far_hop, far_group = [], [], [], []
    for i, (group, source, target, row, ous, slot) in enumerate(far_parts):
        src, dst = source.at[row, ous, ty(0)], target.at[row, ous]
        far_group.append(group)
        far_direct.append(remote(src, dst, far_dev, ("fd", i), ("fg", i)))
        if slot is not None:
            held = passing.at[pl.ds(*slot)]
            far_pass.append(remote(src, held, near_dev, ("fp", i)))
            far_hop.append(remote(held, dst, hop_dev, ("fh", i), ("fg", i)))

    c_parts = ((rows[0], full), (rows[1], head), (rows[1], pl.ds(tx(2), 1)))
    near_c0 = [remote(blocks.at[row, ous, 1], n_c0.at[row, ous], near_dev, ("n0", i))
               for i, (row, ous) in enumerate(c_parts)]
    near_c1 = [remote(blocks.at[row, ous, ty(2)], n_c1.at[row, ous], near_dev, ("n1", i))
               for i, (row, ous) in enumerate(c_parts)]
    far_c0 = [remote(n_c0.at[row, ous], f_c0.at[row, ous], hop_dev, ("f0", i))
              for i, (row, ous) in enumerate(c_parts)]
    near_r = [remote(rhs.at[row, ous, ty(2)], n_r.at[row, ous], near_dev, ("nr", i))
              for i, (row, ous) in enumerate((
                  (rows[0], head), (rows[1], pl.ds(tx(0), 1)), (rows[1], pl.ds(tx(2), 1)),
                  (rows[1], pl.ds(1, 1)), (rows[0], pl.ds(tx(2), 1))))]

    direct_in = [
        remote(rhs.at[rows[0], tx(0), 1], g_r.at[0], inner_dev, "gr0"),
        remote(blocks.at[rows[0], head], g_c.at[0], inner_dev, "gc0"),
        remote(own_m, g_m.at[0], inner_dev, "gm0"),
    ]
    direct_out = [
        remote(rhs.at[rows[1], tx(2), 1], g_r.at[1], outer_dev, "gr1"),
        remote(blocks.at[rows[1], tail], g_c.at[1], outer_dev, "gc1"),
        remote(own_m, g_m.at[1], outer_dev, "gm1"),
    ]
    in_m, in_r, in_c, out_m, out_r, out_mid, out_end = [], [], [], [], [], [], []
    for side, (m, r, coupled) in enumerate(((n_m, n_r, (n_c0, n_c1)), (f_m, f_r, (f_c0, f_c1)))):
        in_m.append(remote(m, d_m.at[0, side], inner_dev, ("im", side)))
        in_r.append(remote(r.at[rows[0], tx(0)], d_r.at[0, side], inner_dev, ("ir", side)))
        out_m.append(remote(m, d_m.at[1, side], outer_dev, ("om", side)))
        out_r.append(remote(r.at[rows[1], tx(2)], d_r.at[1, side], outer_dev, ("or", side)))
        in_c.append([remote(c.at[rows[0], head], d_c.at[0, side, k], inner_dev, ("ic", side, k))
                     for k, c in enumerate(coupled)])
        out_mid.append([remote(c.at[rows[1], 1], d_c.at[1, side, k, 1 - core], outer_dev, ("oc", side, k))
                        for k, c in enumerate(coupled)])
        out_end.append([remote(c.at[rows[1], tx(2)], d_c.at[1, side, k, core], outer_dev, ("oe", side, k))
                        for k, c in enumerate(coupled)])

    local_m = pltpu.make_async_copy(masks, own_masks, local_sem.at[5])
    local_m.start()
    barrier = pltpu.get_barrier_semaphore()
    total = jnp.int32(0)
    peers = [(inside(gx + step, ngx), (gx + step, gy)) for step in (-1, 1)]
    peers += [(inside(gy + step, ngy), (gx, gy + step)) for step in (-2, -1, 1, 2)]
    for exists, device in peers:
        total = total + exists.astype(jnp.int32)

        @pl.when(exists)
        def _(device=device):
            pl.semaphore_signal(barrier, inc=1, device_id=device, device_id_type=MESH)

    pairs = atoms * atoms
    local_m.wait()
    own_m[...] = sum(
        lax.dot_general(
            own_masks[row].astype(F32).reshape(pairs, offsets),
            (lax.broadcasted_iota(jnp.int32, (pairs, 2 * pairs), 0) + pairs * row
             == lax.broadcasted_iota(jnp.int32, (pairs, 2 * pairs), 1)).astype(F32),
            (((0,), (0,)), ((), ())), preferred_element_type=F32)
        for row in (0, 1))
    pl.semaphore_wait(barrier, total)

    def on(condition, actions):
        if condition is None:
            for action in actions:
                action()
        else:
            @pl.when(condition)
            def _():
                for action in actions:
                    action()

    def start(condition, *copies):
        on(condition, [copy.start for copy in copies])

    def arrived(condition, *copies):
        on(condition, [copy.wait_recv for copy in copies])

    def sent(condition, *copies):
        on(condition, [copy.wait_send for copy in copies])

    def is_relayed(i):
        return far_group[i] < mine_relayed

    def start_pass(group):
        for i, copy in enumerate(far_pass):
            if far_group[i] == group:
                start(is_relayed(i), copy)

    def start_direct(i):
        start(both(has_far, jnp.logical_not(is_relayed(i))), far_direct[i])

    def relay(group):
        for i, copy in enumerate(far_pass):
            if far_group[i] == group:
                @pl.when(group < partner_relayed)
                def _(i=i, copy=copy):
                    copy.wait_recv()
                    far_hop[i].start()

    start_pass(0)
    start(None, near_c0[0], n_mask, near_c0[1])
    start_pass(1)
    start(None, near_r[0], near_r[1], near_c1[0], near_c1[1])
    for i in (0, 1, 2, 5):
        start_direct(i)
    start(None, *direct_in)
    start(has_outer, *direct_out)
    start_pass(2)
    start(None, near_c0[2], near_r[2], near_c1[2], near_r[3], near_r[4])
    for i in (6, 3, 4):
        start_direct(i)

    local_c = pltpu.make_async_copy(blocks, own_c, local_sem.at[0])
    own_rhs = ((0, 1, 0, 1), (0, 2, 1, 0), (1, 0, 0, 2), (1, 1, 1, 1))
    local_r = [pltpu.make_async_copy(rhs.at[rows[t], tx(k), 1], o_r.at[i], local_sem.at[1 + i])
               for i, (_, _, t, k) in enumerate(own_rhs)]
    local_n = pltpu.make_async_copy(counts, limits, local_sem.at[6])
    start(None, local_c, local_n, *local_r)

    def clear(*refs):
        for ref in refs:
            ref[...] = jnp.zeros(ref.shape, ref.dtype)

    @pl.when(jnp.logical_not(has_far))
    def _():
        clear(f_c0, f_c1, f_r, f_m, *[d.at[x, 1] for d in (d_c, d_r, d_m) for x in (0, 1)])

    @pl.when(jnp.logical_not(has_outer))
    def _():
        clear(g_c.at[1], g_r.at[1], g_m.at[1], d_c.at[1], d_r.at[1], d_m.at[1])

    wide_shape = (pairs, atoms * b)
    above, across = (lax.broadcasted_iota(jnp.int32, wide_shape, d) for d in (0, 1))
    spread = (above == atoms * (across // b) + across % b // orb).astype(F32)

    def widen(index, packed):
        for row in (0, 1):
            wide[index + row] = product(packed[:, pairs * row:pairs * row + pairs], spread)

    c_refs = (c_of0, c_of1, c_of2, c_of3)
    first_row = (0, 0, 1, 2)

    def put(w, s, k, j, value, mask):
        mask_row = wide[mask, pl.ds(3 * tx(k) + ty(j), 1), :]
        found = near_three(s)
        col = b * ((w + k - 1 - first_row[w]) * len(found) + s + j - 1 - found[0])
        for i in range(atoms):
            masked = value[orb * i:orb * (i + 1)] * mask_row[:, b * i:b * (i + 1)]
            for part, piece in enumerate(split(masked)):
                at = b * part + orb * i
                c_refs[w][s, at:at + orb, col:col + b] = piece

    def put_rhs(solve, u, s, value):
        at = b * (3 * u + s)
        basis[solve, 0, at:at + b, :] = value
        for part, piece in enumerate(split(value)):
            vec[solve, 0, at:at + b, b * part:b * part + b] = piece

    widen(0, own_m[...])
    local_c.wait()
    local_n.wait()
    for t in (0, 1):
        for k in range(3):
            for j in range(3):
                put(1 + t, 1, k, j, own_c[rows[t], tx(k), ty(j)], rows[t])
    for i, (solve, u, _, _) in enumerate(own_rhs):
        local_r[i].wait()
        put_rhs(solve, u, 1, o_r[i])

    arrived(None, *direct_in)
    widen(6, g_m[0])
    for k, slot in ((1, 1 - core), (2, core)):
        for j in range(3):
            put(0, 1, k, j, g_c[0, slot, ty(j)], 6 + core)
    put_rhs(0, 0, 1, g_r[0])

    n_mask.wait_recv()
    start(has_hop, f_mask)
    start(None, in_m[0])
    start(has_outer, out_m[0])
    relay(0)
    widen(2, n_m[...])

    def put_column(s, ref, t, k, j):
        put(1 + t, s, k, j, ref[rows[t], tx(k)], (2 if s == 2 else 4) + rows[t])

    near_c0[0].wait_recv()
    start(has_hop, far_c0[0])
    start(None, in_c[0][0])
    for k in range(3):
        put_column(2, n_c0, 0, k, 1)
    near_c0[1].wait_recv()
    start(has_hop, far_c0[1])
    start(has_outer, out_mid[0][0])
    for k in (0, 1):
        put_column(2, n_c0, 1, k, 1)
    relay(1)
    arrived(None, near_r[0], near_r[1])
    start(None, in_r[0])
    put_rhs(0, 1, 2, n_r[rows[0], 1])
    put_rhs(0, 2, 2, n_r[rows[1], tx(0)])

    arrived(has_far, f_mask)
    start(has_far, in_m[1])
    start(both(has_far, has_outer), out_m[1])
    widen(4, f_m[...])
    arrived(has_far, far_direct[0], far_direct[1])
    start(has_far, in_r[1])
    put_rhs(0, 1, 0, f_r[rows[0], 1])
    put_rhs(0, 2, 0, f_r[rows[1], tx(0)])
    arrived(has_far, far_direct[2])
    start(has_far, in_c[1][1])
    arrived(has_far, far_direct[5])
    start(both(has_far, has_outer), out_mid[1][1])
    for t, ks in ((0, (0, 1, 2)), (1, (0, 1))):
        for k in ks:
            put_column(0, f_c1, t, k, 2)
    arrived(has_far, far_c0[0], far_c0[1])
    start(has_far, in_c[1][0])
    start(both(has_far, has_outer), out_mid[1][0])
    for t, ks in ((0, (0, 1, 2)), (1, (0, 1))):
        for k in ks:
            put_column(0, f_c0, t, k, 1)

    arrived(has_outer, *direct_out)
    widen(8, g_m[1])
    for k, slot in ((1, core), (0, 1 - core)):
        for j in range(3):
            put(3, 1, k, j, g_c[1, slot, ty(j)], 9 - core)
    put_rhs(1, 2, 1, g_r[1])

    near_c1[0].wait_recv()
    start(None, in_c[0][1])
    near_c1[1].wait_recv()
    start(has_outer, out_mid[0][1])
    for t, ks in ((0, (0, 1, 2)), (1, (0, 1))):
        for k in ks:
            put_column(2, n_c1, t, k, 0)

    def put_corner(x, side, ways):
        s = 2 - 2 * side
        for way in ways:
            for k, slot in (((1, 1 - core), (2, core)), ((1, core), (0, 1 - core)))[x]:
                put(3 * x, s, k, 1 if way == 0 else 2 * side, d_c[x, side, way, slot],
                    10 + 2 * (2 * x + side) + (1 - core if x else core))

    for side in (1, 0):
        arrived(side_there[side], in_m[side], in_r[side], *in_c[side])
        widen(10 + 2 * side, d_m[0, side])
        put_corner(0, side, (0, 1))
        put_rhs(0, 0, 2 - 2 * side, d_r[0, side])

    def fold(value):
        return jnp.sum(value.reshape(-1, 8, b), axis=0)

    def column(value):
        return jnp.sum(value, axis=0, keepdims=True)

    def at_of(u, s):
        return slice(b * (3 * u + s), b * (3 * u + s) + b)

    members = [(u, s) for u in range(3) for s in range(3)]

    def apply_row(solve, turn, u, s, only=(0, 1, 2), low=True):
        found = near_three(s)
        used = [k for k in found if k in only]
        if not used:
            return None
        strips = near_three(u)
        ref, first = c_refs[u + solve], strips[0] + solve - first_row[u + solve]
        height = slice(0, 2 * b if low else b)
        if len(used) == len(found):
            left = ref[s, height, b * len(found) * first:b * len(found) * (first + len(strips))]
        else:
            starts = [b * (len(found) * (first + i) + used[0] - found[0]) for i in range(len(strips))]
            left = jnp.concatenate(
                [ref[s, height, at:at + b * len(used)] for at in starts], axis=1)
        right = [vec[solve, turn, b * (3 * k + used[0]):b * (3 * k + used[0] + len(used)), :]
                 for k in strips]
        value = product(left, jnp.concatenate(right, axis=0))
        total = value[0:b, 0:b] + value[0:b, b:2 * b]
        return total + value[b:2 * b, 0:b] if low else total

    def before_near(u, s):
        return () if (u, s) == (2, 2) else (0, 1, 2) if s == 0 else (0, 1)

    def first_product(solve):
        for u, s in members:
            value = apply_row(solve, 0, u, s, before_near(u, s))
            if value is not None:
                basis[solve, 1, at_of(u, s), :] = value

    def rest_of_first(solve, u, s):
        done = before_near(u, s)
        value = apply_row(solve, 0, u, s, tuple(k for k in range(3) if k not in done))
        if not done:
            return value
        partial = basis[solve, 1, at_of(u, s), :]
        return partial if value is None else partial + value

    def solve_cluster(solve, between):
        gram = {}

        def power(j):
            sums = [jnp.zeros((8, b), F32) for _ in range(j + 1)]
            for u, s in members:
                if j == 1 and solve == 1:
                    value = rest_of_first(solve, u, s)
                else:
                    value = apply_row(solve, (j - 1) % 2, u, s)
                basis[solve, j, at_of(u, s), :] = value
                for part, piece in enumerate(split(value)):
                    vec[solve, j % 2, at_of(u, s), b * part:b * part + b] = piece
                for i in range(j):
                    sums[i] = sums[i] + fold(value * basis[solve, i, at_of(u, s), :])
                sums[j] = sums[j] + fold(value * value)
            for i in range(j + 1):
                gram[i, j] = gram[j, i] = column(sums[i])
            between(j)

        def inner(left, other):
            result = None
            for i, a in enumerate(left):
                for k, c in enumerate(other):
                    term = (a * c) * gram[i, k]
                    result = term if result is None else result + term
            return result

        def norm_of(value):
            result = None
            for i, a in enumerate(value):
                for k in range(i, len(value)):
                    term = (a * value[k]) * gram[i, k] * (1.0 if i == k else 2.0)
                    result = term if result is None else result + term
            return jnp.maximum(result, 0.0)

        first_sums = jnp.zeros((8, b), F32)
        for u, s in members:
            value = basis[solve, 0, at_of(u, s), :]
            first_sums = first_sums + fold(value * value)
        gram[0, 0] = column(first_sums)
        count = limits[rows[solve]].astype(F32)
        atom_of = (lax.broadcasted_iota(jnp.int32, (atoms, b), 1) // orb
                   == lax.broadcasted_iota(jnp.int32, (atoms, b), 0)).astype(F32)
        limit = product(jnp.broadcast_to(count, (atoms, atoms)), atom_of)[0:1]

        power(1)
        norm = gram[0, 0]
        shadow = [jnp.ones_like(norm)]
        resid = y_first = shadow
        rho, floor = norm, 0.1 * norm
        tau = jnp.sqrt(norm)
        theta = eta = jnp.zeros_like(norm)
        u_first = along = image(y_first)
        direc, sol = [], []
        for n in range(1, ITERS + 1):
            active = (limit >= float(n)).astype(F32)
            if n > 1:
                power(2 * n - 1)
                rho_next = inner(shadow, resid)
                beta = guarded(rho_next, rho, floor)
                floor = 0.1 * jnp.sqrt(norm * size)
                rho = rho_next
                y_first = add(resid, beta, y_second)
                u_first = image(y_first)
                along = add(u_first, beta, add(u_second, beta, along))
            alpha = guarded(
                rho, inner(shadow, along), 0.1 * jnp.sqrt(norm * (norm_of(along) + 1e-06)))
            ratio = guarded(1.0, alpha, 0.1)
            y_second = add(y_first, -alpha, along)
            u_second = image(y_second)
            for part, (y, u_of) in enumerate(((y_first, u_first), (y_second, u_second))):
                resid = add(resid, -alpha, u_of)
                direc = add(y, theta * theta * eta * ratio, direc)
                if part == 1 and n == ITERS:
                    sums = jnp.zeros((8, b), F32)
                    for u, s in members:
                        value = apply_row(solve, (2 * n - 1) % 2, u, s, low=False)
                        value = value * resid[2 * n]
                        for i in range(2 * n):
                            value = value + basis[solve, i, at_of(u, s), :] * resid[i]
                        sums = sums + fold(value * value)
                    size = column(sums)
                else:
                    if part == 1:
                        power(2 * n)
                    size = norm_of(resid)
                theta = jnp.sqrt(size) / tau
                cosine = 1.0 / jnp.sqrt(1.0 + theta * theta)
                tau = tau * theta * cosine
                eta = cosine * cosine * alpha
                sol = add(sol, active * eta, direc)

        for u, s in members:
            value = basis[solve, 0, at_of(u, s), :] * sol[0]
            for i in range(1, 2 * ITERS):
                value = value + basis[solve, i, at_of(u, s), :] * sol[i]
            out[rows[solve], 3 * tx(u) + ty(s)] = value

    def between(j):
        if j == 1:
            relay(2)
            near_c0[2].wait_recv()
            start(has_hop, far_c0[2])
            start(has_outer, out_end[0][0])
            put_column(2, n_c0, 1, 2, 1)
        if j == 2:
            arrived(has_outer, out_m[0], *out_mid[0])
            arrived(both(has_far, has_outer), out_m[1], *out_mid[1])
            for side in (0, 1):
                widen(14 + 2 * side, d_m[1, side])
            near_r[2].wait_recv()
            start(has_outer, out_r[0])
        if j == 3:
            arrived(has_far, far_direct[6])
            start(both(has_far, has_outer), out_end[1][1])
            put_column(0, f_c1, 1, 2, 2)
        if j == 4:
            near_c1[2].wait_recv()
            start(has_outer, out_end[0][1])
            put_column(2, n_c1, 1, 2, 0)
            arrived(has_far, far_direct[3])
            start(both(has_far, has_outer), out_r[1])
            put_rhs(1, 1, 0, f_r[rows[1], 1])
        if j == 5:
            arrived(has_far, far_c0[2], far_direct[4])
            start(both(has_far, has_outer), out_end[1][0])
            put_column(0, f_c0, 1, 2, 1)
            put_rhs(1, 0, 0, f_r[rows[0], tx(2)])

    solve_cluster(0, between)
    arrived(both(has_far, has_outer), out_r[1], *out_end[1])
    put_corner(1, 1, (0, 1))
    put_rhs(1, 2, 0, d_r[1, 1])
    first_product(1)
    arrived(has_outer, out_r[0], *out_end[0])
    put_corner(1, 0, (0, 1))
    put_rhs(1, 2, 2, d_r[1, 0])
    arrived(None, near_r[3], near_r[4])
    put_rhs(1, 1, 2, n_r[rows[1], 1])
    put_rhs(1, 0, 2, n_r[rows[0], tx(2)])
    solve_cluster(1, lambda j: None)

    sent(None, n_mask, *near_c0, *near_c1, *near_r, *direct_in, in_m[0], in_r[0], *in_c[0])
    sent(has_hop, f_mask, *far_c0)
    for i, copy in enumerate(far_direct):
        sent(both(has_far, jnp.logical_not(is_relayed(i))), copy)
    for i, copy in enumerate(far_pass):
        sent(is_relayed(i), copy)
        sent(far_group[i] < partner_relayed, far_hop[i])
    sent(has_outer, *direct_out)
    for side in (0, 1):
        if side:
            sent(has_far, in_m[1], in_r[1], *in_c[1])
        sent(has_outer if side == 0 else both(has_far, has_outer),
             out_m[side], out_r[side], *out_mid[side], *out_end[side])
    assert all(sum(1 for key in numbers if key[0] == kind) <= COPIES for kind in ("send", "recv"))


def shards(blocks, pair_mask, rhs_rows, counts):
    groups = blocks.shape[0]
    b = blocks.shape[-1]
    atoms = pair_mask.shape[-1]
    offsets = pair_mask.shape[2]
    blocks = blocks.reshape(groups, 3, 3, b, b)
    rhs = rhs_rows.reshape(groups, 3, 3, b, b)
    masks = pair_mask.transpose(0, 1, 3, 4, 2).reshape(groups, atoms, atoms, offsets)
    any_spec = pl.BlockSpec(memory_space=pl.ANY)
    vmem_spec = pl.BlockSpec(memory_space=pltpu.VMEM)

    def raw(*lead):
        return pltpu.VMEM(lead + (b, b), F32)

    def flags(*lead):
        return pltpu.VMEM(lead + (offsets, groups * atoms * atoms), F32)

    solved = pl.pallas_call(
        kernel,
        out_shape=pltpu.VMEM((groups, 9, b, b), F32),
        in_specs=[any_spec, any_spec, any_spec, any_spec],
        out_specs=vmem_spec,
        scratch_shapes=[
            raw(groups, 3, 3), raw(2, 2, 3), raw(groups, 3), raw(groups, 3), raw(groups, 3),
            raw(groups, 3), raw(2, 2, 2, 2), raw(9),
            raw(4), raw(2), raw(groups, 3), raw(groups, 3), raw(2, 2),
            pltpu.VMEM((groups, atoms, atoms, offsets), jnp.int32),
            flags(), flags(), flags(), flags(2), flags(2, 2),
            pltpu.VMEM(counts.shape, jnp.int32),
            pltpu.VMEM((18, offsets, atoms * b), F32),
            pltpu.VMEM((3, 2 * b, 6 * b), BF16),
            pltpu.VMEM((3, 2 * b, 9 * b), BF16),
            pltpu.VMEM((3, 2 * b, 9 * b), BF16),
            pltpu.VMEM((3, 2 * b, 6 * b), BF16),
            pltpu.VMEM((2, 2, 9 * b, 2 * b), BF16),
            pltpu.VMEM((2, 2 * ITERS, 9 * b, b), F32),
            pltpu.SemaphoreType.DMA((COPIES,)),
            pltpu.SemaphoreType.DMA((COPIES,)),
            pltpu.SemaphoreType.DMA((7,)),
        ],
        compiler_params=pltpu.CompilerParams(
            collective_id=0, has_side_effects=True, vmem_limit_bytes=60 * 1024 * 1024
        ),
    )(blocks, masks, rhs, counts)
    return solved.reshape(groups, 1, 9, b, b)


def solution(mesh):
    spec = P("gx", "gy", None, None, None)
    return jax.shard_map(
        shards,
        mesh=mesh,
        in_specs=(spec, spec, spec, P("gx", "gy", None)),
        out_specs=spec,
        check_vma=False,
    )
```

```python
import jax
import jax.numpy as jnp
from jax import lax
from jax.experimental import pallas as pl
from jax.experimental.pallas import tpu as pltpu
from jax.sharding import PartitionSpec as P

ITERS = 3
COPIES = 80
MESH = pl.DeviceIdType.MESH
F32 = jnp.float32
BF16 = jnp.bfloat16
E4M3 = jnp.float8_e4m3fn
E5M2 = jnp.float8_e5m2
C_SCALE = 2.0 ** 21
V_SCALE = 2.0 ** 5


def guarded(top, bottom, floor_val):
    return top * bottom / (bottom * bottom + floor_val * floor_val)


def split(value):
    high = value.astype(BF16)
    return high, (value - high.astype(F32)).astype(BF16)


def product(left, right):
    return jnp.dot(left, right, preferred_element_type=F32)


def near_three(s):
    return range(max(0, s - 1), min(3, s + 2))


def add(left, factor, right):
    result = []
    for k in range(max(len(left), len(right))):
        a = left[k] if k < len(left) else None
        c = right[k] if k < len(right) else None
        if c is None:
            result.append(a)
        else:
            result.append(factor * c if a is None else a + factor * c)
    return result


def image(value):
    return add(list(value) + [None], -1.0, [None] + list(value))


def kernel(
    blocks, masks, rhs, counts, out,
    own_c, g_c, n_c0, n_c1, f_c0, f_c1, d_c, passing,
    o_r, g_r, n_r, f_r, d_r, own_masks, own_m, n_m, f_m, g_m, d_m, limits, wide,
    c_of0, c_of1, c_of2, c_of3, r_of0, r_of1, r_of2, r_of3, vec, coarse, basis,
    send_sem, recv_sem, local_sem,
):
    b = blocks.shape[-1]
    atoms = masks.shape[1]
    offsets = masks.shape[-1]
    orb = b // atoms
    gx, gy = lax.axis_index("gx"), lax.axis_index("gy")
    ngx, ngy = lax.axis_size("gx"), lax.axis_size("gy")
    assert ngx % 2 == 0 and ngy % 2 == 0
    half = ngy // 2
    core, odd = gx % 2, gy % 2
    step_x, step_y = 1 - 2 * core, 1 - 2 * odd
    inner_dev, outer_dev = (gx + step_x, gy), (gx - step_x, gy)
    near_dev, far_dev, hop_dev = (gx, gy + step_y), (gx, gy - step_y), (gx, gy + 2 * step_y)

    def inside(index, size):
        return jnp.logical_and(index >= 0, index < size)

    both = jnp.logical_and
    has_outer = inside(gx - step_x, ngx)
    has_far = inside(gy - step_y, ngy)
    has_hop = inside(gy + 2 * step_y, ngy)
    side_there = (None, has_far)
    rank = jnp.where(odd == 0, gy // 2, half - 1 - gy // 2)
    mine_relayed = (4 * rank) // half
    partner_relayed = (4 * (half - 1 - rank)) // half

    def ty(j):
        return 1 if j == 1 else 2 * odd + step_y * j

    def tx(k):
        return 1 if k == 1 else 2 * (1 - core) - step_x * k

    rows = (1 - core, core)
    head, tail = pl.ds(1 - core, 2), pl.ds(core, 2)
    full = pl.ds(0, 3)

    numbers = {}

    def number(kind, name):
        return numbers.setdefault((kind, name), sum(1 for key in numbers if key[0] == kind))

    def remote(src, dst, device, name, arrival=None):
        return pltpu.make_async_remote_copy(
            src_ref=src, dst_ref=dst, send_sem=send_sem.at[number("send", name)],
            recv_sem=recv_sem.at[number("recv", arrival or name)],
            device_id=device, device_id_type=MESH,
        )

    n_mask = remote(own_m, n_m, near_dev, "nm")
    f_mask = remote(n_m, f_m, hop_dev, "fm")
    low_end, high_end, middle = pl.ds(tx(0), 1), pl.ds(tx(2), 1), pl.ds(1, 1)
    far_parts = (
        (0, rhs, f_r, rows[0], head, (0, 2)), (0, blocks, f_c1, rows[1], high_end, (2, 1)),
        (1, blocks, f_c1, rows[1], head, (3, 2)), (1, rhs, f_r, rows[0], high_end, (5, 1)),
        (2, blocks, f_c1, rows[0], head, (6, 2)), (2, rhs, f_r, rows[1], high_end, (8, 1)),
        (4, blocks, f_c1, rows[0], high_end, None), (4, rhs, f_r, rows[1], low_end, None),
        (4, rhs, f_r, rows[1], middle, None),
    )
    far_direct, far_pass, far_hop, far_group = [], [], [], []
    for i, (group, source, target, row, ous, slot) in enumerate(far_parts):
        src, dst = source.at[row, ous, ty(0)], target.at[row, ous]
        far_group.append(group)
        far_direct.append(remote(src, dst, far_dev, ("fd", i), ("fg", i)))
        if slot is not None:
            held = passing.at[pl.ds(*slot)]
            far_pass.append(remote(src, held, near_dev, ("fp", i)))
            far_hop.append(remote(held, dst, hop_dev, ("fh", i), ("fg", i)))

    c_parts = ((rows[0], full), (rows[1], head), (rows[1], pl.ds(tx(2), 1)))
    near_c0 = [remote(blocks.at[row, ous, 1], n_c0.at[row, ous], near_dev, ("n0", i))
               for i, (row, ous) in enumerate(c_parts)]
    near_c1 = [remote(blocks.at[row, ous, ty(2)], n_c1.at[row, ous], near_dev, ("n1", i))
               for i, (row, ous) in enumerate(c_parts)]
    far_c0 = [remote(n_c0.at[row, ous], f_c0.at[row, ous], hop_dev, ("f0", i))
              for i, (row, ous) in enumerate(c_parts)]
    near_r = [remote(rhs.at[row, ous, ty(2)], n_r.at[row, ous], near_dev, ("nr", i))
              for i, (row, ous) in enumerate((
                  (rows[0], head), (rows[1], pl.ds(tx(0), 1)), (rows[1], pl.ds(tx(2), 1)),
                  (rows[1], pl.ds(1, 1)), (rows[0], pl.ds(tx(2), 1))))]

    direct_in = [
        remote(rhs.at[rows[0], tx(0), 1], g_r.at[0], inner_dev, "gr0"),
        remote(blocks.at[rows[0], head], g_c.at[0], inner_dev, "gc0"),
        remote(own_m, g_m.at[0], inner_dev, "gm0"),
    ]
    direct_out = [
        remote(rhs.at[rows[1], tx(2), 1], g_r.at[1], outer_dev, "gr1"),
        remote(blocks.at[rows[1], tail], g_c.at[1], outer_dev, "gc1"),
        remote(own_m, g_m.at[1], outer_dev, "gm1"),
    ]
    in_m, in_r, in_c, out_m, out_r, out_mid, out_end = [], [], [], [], [], [], []
    for side, (m, r, coupled) in enumerate(((n_m, n_r, (n_c0, n_c1)), (f_m, f_r, (f_c0, f_c1)))):
        in_m.append(remote(m, d_m.at[0, side], inner_dev, ("im", side)))
        in_r.append(remote(r.at[rows[0], tx(0)], d_r.at[0, side], inner_dev, ("ir", side)))
        out_m.append(remote(m, d_m.at[1, side], outer_dev, ("om", side)))
        out_r.append(remote(r.at[rows[1], tx(2)], d_r.at[1, side], outer_dev, ("or", side)))
        in_c.append([remote(c.at[rows[0], head], d_c.at[0, side, k], inner_dev, ("ic", side, k))
                     for k, c in enumerate(coupled)])
        out_mid.append([remote(c.at[rows[1], 1], d_c.at[1, side, k, 1 - core], outer_dev, ("oc", side, k))
                        for k, c in enumerate(coupled)])
        out_end.append([remote(c.at[rows[1], tx(2)], d_c.at[1, side, k, core], outer_dev, ("oe", side, k))
                        for k, c in enumerate(coupled)])

    local_m = pltpu.make_async_copy(masks, own_masks, local_sem.at[5])
    local_m.start()
    barrier = pltpu.get_barrier_semaphore()
    total = jnp.int32(0)
    peers = [(inside(gx + step, ngx), (gx + step, gy)) for step in (-1, 1)]
    peers += [(inside(gy + step, ngy), (gx, gy + step)) for step in (-2, -1, 1, 2)]
    for exists, device in peers:
        total = total + exists.astype(jnp.int32)

        @pl.when(exists)
        def _(device=device):
            pl.semaphore_signal(barrier, inc=1, device_id=device, device_id_type=MESH)

    pairs = atoms * atoms
    local_m.wait()
    own_m[...] = sum(
        lax.dot_general(
            own_masks[row].astype(F32).reshape(pairs, offsets),
            (lax.broadcasted_iota(jnp.int32, (pairs, 2 * pairs), 0) + pairs * row
             == lax.broadcasted_iota(jnp.int32, (pairs, 2 * pairs), 1)).astype(F32),
            (((0,), (0,)), ((), ())), preferred_element_type=F32)
        for row in (0, 1))
    pl.semaphore_wait(barrier, total)

    def on(condition, actions):
        if condition is None:
            for action in actions:
                action()
        else:
            @pl.when(condition)
            def _():
                for action in actions:
                    action()

    def start(condition, *copies):
        on(condition, [copy.start for copy in copies])

    def arrived(condition, *copies):
        on(condition, [copy.wait_recv for copy in copies])

    def sent(condition, *copies):
        on(condition, [copy.wait_send for copy in copies])

    def is_relayed(i):
        return far_group[i] < mine_relayed

    def start_pass(*items):
        for i in items:
            start(is_relayed(i), far_pass[i])

    def start_direct(i):
        start(both(has_far, jnp.logical_not(is_relayed(i))), far_direct[i])

    def relay(*items):
        for i in items:
            @pl.when(far_group[i] < partner_relayed)
            def _(i=i):
                far_pass[i].wait_recv()
                far_hop[i].start()

    start_pass(0)
    start(None, near_c0[0], n_mask, near_c0[1])
    start_pass(2, 4)
    start(None, near_r[0], near_r[1], near_c1[0], near_c1[1])
    for i in (0, 7, 4, 6, 2):
        start_direct(i)
    start(None, *direct_in)
    start(has_outer, *direct_out)
    start_pass(1, 5, 3)
    start(None, near_c0[2], near_r[2], near_c1[2], near_r[3], near_r[4])
    for i in (1, 5, 8, 3):
        start_direct(i)

    local_c = pltpu.make_async_copy(blocks, own_c, local_sem.at[0])
    own_rhs = ((0, 1, 0, 1), (0, 2, 1, 0), (1, 0, 0, 2), (1, 1, 1, 1))
    local_r = [pltpu.make_async_copy(rhs.at[rows[t], tx(k), 1], o_r.at[i], local_sem.at[1 + i])
               for i, (_, _, t, k) in enumerate(own_rhs)]
    local_n = pltpu.make_async_copy(counts, limits, local_sem.at[6])
    start(None, local_c, local_n, *local_r)

    def clear(*refs):
        for ref in refs:
            ref[...] = jnp.zeros(ref.shape, ref.dtype)

    @pl.when(jnp.logical_not(has_far))
    def _():
        clear(f_c0, f_c1, f_r, f_m, *[d.at[x, 1] for d in (d_c, d_r, d_m) for x in (0, 1)])

    @pl.when(jnp.logical_not(has_outer))
    def _():
        clear(g_c.at[1], g_r.at[1], g_m.at[1], d_c.at[1], d_r.at[1], d_m.at[1])

    wide_shape = (pairs, atoms * b)
    above, across = (lax.broadcasted_iota(jnp.int32, wide_shape, d) for d in (0, 1))
    spread = (above == atoms * (across // b) + across % b // orb).astype(F32)

    def widen(index, packed):
        for row in (0, 1):
            wide[index + row] = product(packed[:, pairs * row:pairs * row + pairs], spread)

    c_refs = (c_of0, c_of1, c_of2, c_of3)
    r_refs = (r_of0, r_of1, r_of2, r_of3)
    first_row = (0, 0, 1, 2)

    def put(w, s, k, j, value, mask):
        mask_row = wide[mask, pl.ds(3 * tx(k) + ty(j), 1), :]
        found = near_three(s)
        col = b * ((w + k - 1 - first_row[w]) * len(found) + s + j - 1 - found[0])
        masked = jnp.concatenate(
            [value[orb * i:orb * (i + 1)] * mask_row[:, b * i:b * (i + 1)] for i in range(atoms)],
            axis=0)
        high = masked.astype(BF16)
        rest = masked - high.astype(F32)
        c_refs[w][s, 0:b, col:col + b] = high
        c_refs[w][s, b:2 * b, col:col + b] = rest.astype(BF16)
        r_refs[w][s, :, col:col + b] = (rest * C_SCALE).astype(E4M3)

    def put_rhs(solve, u, s, value):
        at = b * (3 * u + s)
        basis[solve, 0, at:at + b, :] = value
        for part, piece in enumerate(split(value)):
            vec[solve, 0, at:at + b, b * part:b * part + b] = piece

    widen(0, own_m[...])
    local_c.wait()
    local_n.wait()
    for t in (0, 1):
        for k in range(3):
            for j in range(3):
                put(1 + t, 1, k, j, own_c[rows[t], tx(k), ty(j)], rows[t])
    for i, (solve, u, _, _) in enumerate(own_rhs):
        local_r[i].wait()
        put_rhs(solve, u, 1, o_r[i])

    arrived(None, *direct_in)
    widen(6, g_m[0])
    for k, slot in ((1, 1 - core), (2, core)):
        for j in range(3):
            put(0, 1, k, j, g_c[0, slot, ty(j)], 6 + core)
    put_rhs(0, 0, 1, g_r[0])

    n_mask.wait_recv()
    start(has_hop, f_mask)
    start(None, in_m[0])
    start(has_outer, out_m[0])
    relay(0)
    widen(2, n_m[...])

    def put_column(s, ref, t, k, j):
        put(1 + t, s, k, j, ref[rows[t], tx(k)], (2 if s == 2 else 4) + rows[t])

    near_c0[0].wait_recv()
    start(has_hop, far_c0[0])
    start(None, in_c[0][0])
    for k in range(3):
        put_column(2, n_c0, 0, k, 1)
    near_c0[1].wait_recv()
    start(has_hop, far_c0[1])
    start(has_outer, out_mid[0][0])
    for k in (0, 1):
        put_column(2, n_c0, 1, k, 1)
    relay(2, 4)
    arrived(None, near_r[0], near_r[1])
    start(None, in_r[0])
    put_rhs(0, 1, 2, n_r[rows[0], 1])
    put_rhs(0, 2, 2, n_r[rows[1], tx(0)])

    arrived(has_far, f_mask)
    start(has_far, in_m[1])
    start(both(has_far, has_outer), out_m[1])
    widen(4, f_m[...])
    arrived(has_far, far_direct[0], far_direct[7])
    start(has_far, in_r[1])
    put_rhs(0, 1, 0, f_r[rows[0], 1])
    put_rhs(0, 2, 0, f_r[rows[1], tx(0)])
    arrived(has_far, far_direct[4])
    start(has_far, in_c[1][1])
    arrived(has_far, far_direct[6], far_direct[2])
    start(both(has_far, has_outer), out_mid[1][1])
    for t, ks in ((0, (0, 1, 2)), (1, (0, 1))):
        for k in ks:
            put_column(0, f_c1, t, k, 2)
    arrived(has_far, far_c0[0], far_c0[1])
    start(has_far, in_c[1][0])
    start(both(has_far, has_outer), out_mid[1][0])
    for t, ks in ((0, (0, 1, 2)), (1, (0, 1))):
        for k in ks:
            put_column(0, f_c0, t, k, 1)

    arrived(has_outer, *direct_out)
    widen(8, g_m[1])
    for k, slot in ((1, core), (0, 1 - core)):
        for j in range(3):
            put(3, 1, k, j, g_c[1, slot, ty(j)], 9 - core)
    put_rhs(1, 2, 1, g_r[1])

    near_c1[0].wait_recv()
    start(None, in_c[0][1])
    near_c1[1].wait_recv()
    start(has_outer, out_mid[0][1])
    for t, ks in ((0, (0, 1, 2)), (1, (0, 1))):
        for k in ks:
            put_column(2, n_c1, t, k, 0)

    def put_corner(x, side, ways):
        s = 2 - 2 * side
        for way in ways:
            for k, slot in (((1, 1 - core), (2, core)), ((1, core), (0, 1 - core)))[x]:
                put(3 * x, s, k, 1 if way == 0 else 2 * side, d_c[x, side, way, slot],
                    10 + 2 * (2 * x + side) + (1 - core if x else core))

    for side in (1, 0):
        arrived(side_there[side], in_m[side], in_r[side], *in_c[side])
        widen(10 + 2 * side, d_m[0, side])
        put_corner(0, side, (0, 1))
        put_rhs(0, 0, 2 - 2 * side, d_r[0, side])

    def fold(value):
        return jnp.sum(value.reshape(-1, 8, b), axis=0)

    def column(value):
        return jnp.sum(value, axis=0, keepdims=True)

    def at_of(u, s):
        return slice(b * (3 * u + s), b * (3 * u + s) + b)

    members = [(u, s) for u in range(3) for s in range(3)]

    def apply_row(solve, turn, u, s, only=(0, 1, 2), low=True, scale=None):
        found = near_three(s)
        used = [k for k in found if k in only]
        if not used:
            return None
        strips = near_three(u)
        ref, first = c_refs[u + solve], strips[0] + solve - first_row[u + solve]
        height = slice(0, 2 * b if low else b)
        if len(used) == len(found):
            left = ref[s, height, b * len(found) * first:b * len(found) * (first + len(strips))]
        else:
            starts = [b * (len(found) * (first + i) + used[0] - found[0]) for i in range(len(strips))]
            left = jnp.concatenate(
                [ref[s, height, at:at + b * len(used)] for at in starts], axis=1)
        right = [vec[solve, turn, b * (3 * k + used[0]):b * (3 * k + used[0] + len(used)), :]
                 for k in strips]
        value = product(left, jnp.concatenate(right, axis=0))
        total = value[0:b, 0:b] + value[0:b, b:2 * b]
        if scale is not None:
            lanes = slice(b * len(found) * first, b * len(found) * (first + len(strips)))
            right = [coarse[solve, turn, b * (3 * k + found[0]):b * (3 * k + found[0] + len(found)), :]
                     for k in strips]
            return total + scale * product(
                r_refs[u + solve][s, :, lanes], jnp.concatenate(right, axis=0))
        return total + value[b:2 * b, 0:b] if low else total

    def before_near(u, s):
        return () if (u, s) == (2, 2) else (0, 1, 2) if s == 0 else (0, 1)

    def first_product(solve):
        for u, s in members:
            value = apply_row(solve, 0, u, s, before_near(u, s))
            if value is not None:
                basis[solve, 1, at_of(u, s), :] = value

    def rest_of_first(solve, u, s):
        done = before_near(u, s)
        value = apply_row(solve, 0, u, s, tuple(k for k in range(3) if k not in done))
        if not done:
            return value
        partial = basis[solve, 1, at_of(u, s), :]
        return partial if value is None else partial + value

    def solve_cluster(solve, between):
        gram = {}
        lengths = {}

        def power(j):
            square = gram[j - 1, j - 1]
            inverse = jnp.where(square > 0.0, lax.rsqrt(square), 0.0)
            lengths[j - 1] = square * inverse
            shrink = V_SCALE * inverse
            sums = [jnp.zeros((8, b), F32) for _ in range(j + 1)]
            for u, s in members:
                if j == 1 and solve == 1:
                    value = rest_of_first(solve, u, s)
                else:
                    scale = None if j == 1 else lengths[j - 2] * (1.0 / (C_SCALE * V_SCALE))
                    value = apply_row(solve, (j - 1) % 2, u, s, low=j == 1, scale=scale)
                basis[solve, j, at_of(u, s), :] = value
                if j < 2 * ITERS - 1:
                    coarse[solve, j % 2, at_of(u, s), :] = (value * shrink).astype(E5M2)
                for part, piece in enumerate(split(value)):
                    vec[solve, j % 2, at_of(u, s), b * part:b * part + b] = piece
                for i in range(j):
                    sums[i] = sums[i] + fold(value * basis[solve, i, at_of(u, s), :])
                sums[j] = sums[j] + fold(value * value)
            for i in range(j + 1):
                gram[i, j] = gram[j, i] = column(sums[i])
            between(j)

        def inner(left, other):
            result = None
            for i, a in enumerate(left):
                for k, c in enumerate(other):
                    term = (a * c) * gram[i, k]
                    result = term if result is None else result + term
            return result

        def norm_of(value):
            result = None
            for i, a in enumerate(value):
                for k in range(i, len(value)):
                    term = (a * value[k]) * gram[i, k] * (1.0 if i == k else 2.0)
                    result = term if result is None else result + term
            return jnp.maximum(result, 0.0)

        first_sums = jnp.zeros((8, b), F32)
        for u, s in members:
            value = basis[solve, 0, at_of(u, s), :]
            first_sums = first_sums + fold(value * value)
        gram[0, 0] = column(first_sums)
        count = limits[rows[solve]].astype(F32)
        atom_of = (lax.broadcasted_iota(jnp.int32, (atoms, b), 1) // orb
                   == lax.broadcasted_iota(jnp.int32, (atoms, b), 0)).astype(F32)
        limit = product(jnp.broadcast_to(count, (atoms, atoms)), atom_of)[0:1]

        power(1)
        norm = gram[0, 0]
        shadow = [jnp.ones_like(norm)]
        resid = y_first = shadow
        rho, floor = norm, 0.1 * norm
        tau = jnp.sqrt(norm)
        theta = eta = jnp.zeros_like(norm)
        u_first = along = image(y_first)
        direc, sol = [], []
        for n in range(1, ITERS + 1):
            active = (limit >= float(n)).astype(F32)
            if n > 1:
                power(2 * n - 1)
                rho_next = inner(shadow, resid)
                beta = guarded(rho_next, rho, floor)
                floor = 0.1 * jnp.sqrt(norm * size)
                rho = rho_next
                y_first = add(resid, beta, y_second)
                u_first = image(y_first)
                along = add(u_first, beta, add(u_second, beta, along))
            alpha = guarded(
                rho, inner(shadow, along), 0.1 * jnp.sqrt(norm * (norm_of(along) + 1e-06)))
            ratio = guarded(1.0, alpha, 0.1)
            y_second = add(y_first, -alpha, along)
            u_second = image(y_second)
            for part, (y, u_of) in enumerate(((y_first, u_first), (y_second, u_second))):
                resid = add(resid, -alpha, u_of)
                direc = add(y, theta * theta * eta * ratio, direc)
                if part == 1 and n == ITERS:
                    sums = jnp.zeros((8, b), F32)
                    for u, s in members:
                        value = apply_row(solve, (2 * n - 1) % 2, u, s, low=False)
                        value = value * resid[2 * n]
                        for i in range(2 * n):
                            value = value + basis[solve, i, at_of(u, s), :] * resid[i]
                        sums = sums + fold(value * value)
                    size = column(sums)
                else:
                    if part == 1:
                        power(2 * n)
                    size = norm_of(resid)
                theta = jnp.sqrt(size) / tau
                cosine = 1.0 / jnp.sqrt(1.0 + theta * theta)
                tau = tau * theta * cosine
                eta = cosine * cosine * alpha
                sol = add(sol, active * eta, direc)

        for u, s in members:
            value = basis[solve, 0, at_of(u, s), :] * sol[0]
            for i in range(1, 2 * ITERS):
                value = value + basis[solve, i, at_of(u, s), :] * sol[i]
            out[rows[solve], 3 * tx(u) + ty(s)] = value

    def between(j):
        if j == 1:
            relay(1, 5, 3)
            near_c0[2].wait_recv()
            start(has_hop, far_c0[2])
            start(has_outer, out_end[0][0])
            put_column(2, n_c0, 1, 2, 1)
        if j == 2:
            arrived(has_outer, out_m[0], *out_mid[0])
            arrived(both(has_far, has_outer), out_m[1], *out_mid[1])
            for side in (0, 1):
                widen(14 + 2 * side, d_m[1, side])
            near_r[2].wait_recv()
            start(has_outer, out_r[0])
        if j == 3:
            arrived(has_far, far_direct[1])
            start(both(has_far, has_outer), out_end[1][1])
            put_column(0, f_c1, 1, 2, 2)
        if j == 4:
            near_c1[2].wait_recv()
            start(has_outer, out_end[0][1])
            put_column(2, n_c1, 1, 2, 0)
            arrived(has_far, far_direct[5], far_direct[8])
            start(both(has_far, has_outer), out_r[1])
            put_rhs(1, 1, 0, f_r[rows[1], 1])
        if j == 5:
            arrived(has_far, far_c0[2], far_direct[3])
            start(both(has_far, has_outer), out_end[1][0])
            put_column(0, f_c0, 1, 2, 1)
            put_rhs(1, 0, 0, f_r[rows[0], tx(2)])

    solve_cluster(0, between)
    arrived(both(has_far, has_outer), out_r[1], *out_end[1])
    put_corner(1, 1, (0, 1))
    put_rhs(1, 2, 0, d_r[1, 1])
    first_product(1)
    arrived(has_outer, out_r[0], *out_end[0])
    put_corner(1, 0, (0, 1))
    put_rhs(1, 2, 2, d_r[1, 0])
    arrived(None, near_r[3], near_r[4])
    put_rhs(1, 1, 2, n_r[rows[1], 1])
    put_rhs(1, 0, 2, n_r[rows[0], tx(2)])
    solve_cluster(1, lambda j: None)

    sent(None, n_mask, *near_c0, *near_c1, *near_r, *direct_in, in_m[0], in_r[0], *in_c[0])
    sent(has_hop, f_mask, *far_c0)
    for i, copy in enumerate(far_direct):
        sent(both(has_far, jnp.logical_not(is_relayed(i))), copy)
    for i, copy in enumerate(far_pass):
        sent(is_relayed(i), copy)
        sent(far_group[i] < partner_relayed, far_hop[i])
    sent(has_outer, *direct_out)
    for side in (0, 1):
        if side:
            sent(has_far, in_m[1], in_r[1], *in_c[1])
        sent(has_outer if side == 0 else both(has_far, has_outer),
             out_m[side], out_r[side], *out_mid[side], *out_end[side])
    assert all(sum(1 for key in numbers if key[0] == kind) <= COPIES for kind in ("send", "recv"))


def shards(blocks, pair_mask, rhs_rows, counts):
    groups = blocks.shape[0]
    b = blocks.shape[-1]
    atoms = pair_mask.shape[-1]
    offsets = pair_mask.shape[2]
    blocks = blocks.reshape(groups, 3, 3, b, b)
    rhs = rhs_rows.reshape(groups, 3, 3, b, b)
    masks = pair_mask.transpose(0, 1, 3, 4, 2).reshape(groups, atoms, atoms, offsets)
    any_spec = pl.BlockSpec(memory_space=pl.ANY)
    vmem_spec = pl.BlockSpec(memory_space=pltpu.VMEM)

    def raw(*lead):
        return pltpu.VMEM(lead + (b, b), F32)

    def flags(*lead):
        return pltpu.VMEM(lead + (offsets, groups * atoms * atoms), F32)

    solved = pl.pallas_call(
        kernel,
        out_shape=pltpu.VMEM((groups, 9, b, b), F32),
        in_specs=[any_spec, any_spec, any_spec, any_spec],
        out_specs=vmem_spec,
        scratch_shapes=[
            raw(groups, 3, 3), raw(2, 2, 3), raw(groups, 3), raw(groups, 3), raw(groups, 3),
            raw(groups, 3), raw(2, 2, 2, 2), raw(9),
            raw(4), raw(2), raw(groups, 3), raw(groups, 3), raw(2, 2),
            pltpu.VMEM((groups, atoms, atoms, offsets), jnp.int32),
            flags(), flags(), flags(), flags(2), flags(2, 2),
            pltpu.VMEM(counts.shape, jnp.int32),
            pltpu.VMEM((18, offsets, atoms * b), F32),
            pltpu.VMEM((3, 2 * b, 6 * b), BF16),
            pltpu.VMEM((3, 2 * b, 9 * b), BF16),
            pltpu.VMEM((3, 2 * b, 9 * b), BF16),
            pltpu.VMEM((3, 2 * b, 6 * b), BF16),
            pltpu.VMEM((3, b, 6 * b), E4M3),
            pltpu.VMEM((3, b, 9 * b), E4M3),
            pltpu.VMEM((3, b, 9 * b), E4M3),
            pltpu.VMEM((3, b, 6 * b), E4M3),
            pltpu.VMEM((2, 2, 9 * b, 2 * b), BF16),
            pltpu.VMEM((2, 2, 9 * b, b), E5M2),
            pltpu.VMEM((2, 2 * ITERS, 9 * b, b), F32),
            pltpu.SemaphoreType.DMA((COPIES,)),
            pltpu.SemaphoreType.DMA((COPIES,)),
            pltpu.SemaphoreType.DMA((7,)),
        ],
        compiler_params=pltpu.CompilerParams(
            collective_id=0, has_side_effects=True, vmem_limit_bytes=60 * 1024 * 1024
        ),
    )(blocks, masks, rhs, counts)
    return solved.reshape(groups, 1, 9, b, b)


def solution(mesh):
    spec = P("gx", "gy", None, None, None)
    return jax.shard_map(
        shards,
        mesh=mesh,
        in_specs=(spec, spec, spec, P("gx", "gy", None)),
        out_specs=spec,
        check_vma=False,
    )
```

```python
import jax
import jax.numpy as jnp
from jax import lax
from jax.experimental import pallas as pl
from jax.experimental.pallas import tpu as pltpu
from jax.sharding import PartitionSpec as P

ITERS = 3
COPIES = 80
MESH = pl.DeviceIdType.MESH
F32 = jnp.float32
BF16 = jnp.bfloat16
E4M3 = jnp.float8_e4m3fn
E5M2 = jnp.float8_e5m2
C_SCALE = 2.0 ** 21
V_SCALE = 2.0 ** 5


def guarded(top, bottom, floor_val):
    return top * bottom / (bottom * bottom + floor_val * floor_val)


def split(value):
    high = value.astype(BF16)
    return high, (value - high.astype(F32)).astype(BF16)


def product(left, right):
    return jnp.dot(left, right, preferred_element_type=F32)


def near_three(s):
    return range(max(0, s - 1), min(3, s + 2))


def add(left, factor, right):
    result = []
    for k in range(max(len(left), len(right))):
        a = left[k] if k < len(left) else None
        c = right[k] if k < len(right) else None
        if c is None:
            result.append(a)
        else:
            result.append(factor * c if a is None else a + factor * c)
    return result


def image(value):
    return add(list(value) + [None], -1.0, [None] + list(value))


def kernel(
    blocks, masks, rhs, counts, out,
    own_c, g_c, n_c0, n_c1, f_c0, f_c1, d_c, passing,
    o_r, g_r, n_r, f_r, d_r, own_masks, own_m, n_m, f_m, g_m, d_m, limits, wide,
    c_of0, c_of1, c_of2, c_of3, r_of0, r_of1, r_of2, r_of3, vec, coarse, basis,
    send_sem, recv_sem, local_sem,
):
    b = blocks.shape[-1]
    atoms = masks.shape[1]
    offsets = masks.shape[-1]
    orb = b // atoms
    gx, gy = lax.axis_index("gx"), lax.axis_index("gy")
    ngx, ngy = lax.axis_size("gx"), lax.axis_size("gy")
    assert ngx % 2 == 0 and ngy % 2 == 0
    half = ngy // 2
    core, odd = gx % 2, gy % 2
    step_x, step_y = 1 - 2 * core, 1 - 2 * odd
    inner_dev, outer_dev = (gx + step_x, gy), (gx - step_x, gy)
    near_dev, far_dev, hop_dev = (gx, gy + step_y), (gx, gy - step_y), (gx, gy + 2 * step_y)

    def inside(index, size):
        return jnp.logical_and(index >= 0, index < size)

    both = jnp.logical_and
    has_outer = inside(gx - step_x, ngx)
    has_far = inside(gy - step_y, ngy)
    has_hop = inside(gy + 2 * step_y, ngy)
    rank = jnp.where(odd == 0, gy // 2, half - 1 - gy // 2)
    mine_relayed = (4 * rank) // half
    partner_relayed = (4 * (half - 1 - rank)) // half

    def ty(j):
        return 1 if j == 1 else 2 * odd + step_y * j

    def tx(k):
        return 1 if k == 1 else 2 * (1 - core) - step_x * k

    rows = (1 - core, core)
    head, tail = pl.ds(1 - core, 2), pl.ds(core, 2)
    full = pl.ds(0, 3)

    numbers = {}

    def number(kind, name):
        return numbers.setdefault((kind, name), sum(1 for key in numbers if key[0] == kind))

    def remote(src, dst, device, name, arrival=None):
        return pltpu.make_async_remote_copy(
            src_ref=src, dst_ref=dst, send_sem=send_sem.at[number("send", name)],
            recv_sem=recv_sem.at[number("recv", arrival or name)],
            device_id=device, device_id_type=MESH,
        )

    n_mask = remote(own_m, n_m, near_dev, "nm")
    f_mask = remote(n_m, f_m, hop_dev, "fm")
    low_end, high_end, middle = pl.ds(tx(0), 1), pl.ds(tx(2), 1), pl.ds(1, 1)
    far_parts = (
        (0, rhs, f_r, rows[0], head, (0, 2)), (0, blocks, f_c1, rows[1], high_end, (2, 1)),
        (1, blocks, f_c1, rows[1], head, (3, 2)), (1, rhs, f_r, rows[0], high_end, (5, 1)),
        (2, blocks, f_c1, rows[0], head, (6, 2)), (2, rhs, f_r, rows[1], high_end, (8, 1)),
        (4, blocks, f_c1, rows[0], high_end, None), (4, rhs, f_r, rows[1], low_end, None),
        (4, rhs, f_r, rows[1], middle, None),
    )
    far_direct, far_pass, far_hop, far_group = [], [], [], []
    for i, (group, source, target, row, ous, slot) in enumerate(far_parts):
        src, dst = source.at[row, ous, ty(0)], target.at[row, ous]
        far_group.append(group)
        far_direct.append(remote(src, dst, far_dev, ("fd", i), ("fg", i)))
        if slot is not None:
            held = passing.at[pl.ds(*slot)]
            far_pass.append(remote(src, held, near_dev, ("fp", i)))
            far_hop.append(remote(held, dst, hop_dev, ("fh", i), ("fg", i)))

    c_parts = ((rows[0], full), (rows[1], head), (rows[1], pl.ds(tx(2), 1)))
    near_c0 = [remote(blocks.at[row, ous, 1], n_c0.at[row, ous], near_dev, ("n0", i))
               for i, (row, ous) in enumerate(c_parts)]
    near_c1 = [remote(blocks.at[row, ous, ty(2)], n_c1.at[row, ous], near_dev, ("n1", i))
               for i, (row, ous) in enumerate(c_parts)]
    far_c0 = [remote(n_c0.at[row, ous], f_c0.at[row, ous], hop_dev, ("f0", i))
              for i, (row, ous) in enumerate(c_parts)]
    near_r = [remote(rhs.at[row, ous, ty(2)], n_r.at[row, ous], near_dev, ("nr", i))
              for i, (row, ous) in enumerate((
                  (rows[0], head), (rows[1], pl.ds(tx(0), 1)), (rows[1], pl.ds(tx(2), 1)),
                  (rows[1], pl.ds(1, 1)), (rows[0], pl.ds(tx(2), 1))))]

    direct_in = [
        remote(rhs.at[rows[0], tx(0), 1], g_r.at[0], inner_dev, "gr0"),
        remote(blocks.at[rows[0], head], g_c.at[0], inner_dev, "gc0"),
        remote(own_m, g_m.at[0], inner_dev, "gm0"),
    ]
    direct_out = [
        remote(rhs.at[rows[1], tx(2), 1], g_r.at[1], outer_dev, "gr1"),
        remote(blocks.at[rows[1], tail], g_c.at[1], outer_dev, "gc1"),
        remote(own_m, g_m.at[1], outer_dev, "gm1"),
    ]
    in_m, in_r, in_c, out_m, out_r, out_mid, out_end = [], [], [], [], [], [], []
    for side, (m, r, coupled) in enumerate(((n_m, n_r, (n_c0, n_c1)), (f_m, f_r, (f_c0, f_c1)))):
        in_m.append(remote(m, d_m.at[0, side], inner_dev, ("im", side)))
        in_r.append(remote(r.at[rows[0], tx(0)], d_r.at[0, side], inner_dev, ("ir", side)))
        out_m.append(remote(m, d_m.at[1, side], outer_dev, ("om", side)))
        out_r.append(remote(r.at[rows[1], tx(2)], d_r.at[1, side], outer_dev, ("or", side)))
        in_c.append([remote(c.at[rows[0], head], d_c.at[0, side, k], inner_dev, ("ic", side, k))
                     for k, c in enumerate(coupled)])
        out_mid.append([remote(c.at[rows[1], 1], d_c.at[1, side, k, 1 - core], outer_dev, ("oc", side, k))
                        for k, c in enumerate(coupled)])
        out_end.append([remote(c.at[rows[1], tx(2)], d_c.at[1, side, k, core], outer_dev, ("oe", side, k))
                        for k, c in enumerate(coupled)])

    local_m = pltpu.make_async_copy(masks, own_masks, local_sem.at[5])
    local_m.start()
    barrier = pltpu.get_barrier_semaphore()
    total = jnp.int32(0)
    peers = [(inside(gx + step, ngx), (gx + step, gy)) for step in (-1, 1)]
    peers += [(inside(gy + step, ngy), (gx, gy + step)) for step in (-2, -1, 1, 2)]
    for exists, device in peers:
        total = total + exists.astype(jnp.int32)

        @pl.when(exists)
        def _(device=device):
            pl.semaphore_signal(barrier, inc=1, device_id=device, device_id_type=MESH)

    pairs = atoms * atoms
    local_m.wait()
    own_m[...] = sum(
        lax.dot_general(
            own_masks[row].astype(F32).reshape(pairs, offsets),
            (lax.broadcasted_iota(jnp.int32, (pairs, 2 * pairs), 0) + pairs * row
             == lax.broadcasted_iota(jnp.int32, (pairs, 2 * pairs), 1)).astype(F32),
            (((0,), (0,)), ((), ())), preferred_element_type=F32)
        for row in (0, 1))
    pl.semaphore_wait(barrier, total)

    def on(condition, actions):
        if condition is None:
            for action in actions:
                action()
        else:
            @pl.when(condition)
            def _():
                for action in actions:
                    action()

    def start(condition, *copies):
        on(condition, [copy.start for copy in copies])

    def arrived(condition, *copies):
        on(condition, [copy.wait_recv for copy in copies])

    def sent(condition, *copies):
        on(condition, [copy.wait_send for copy in copies])

    def is_relayed(i):
        return far_group[i] < mine_relayed

    def start_pass(*items):
        for i in items:
            start(is_relayed(i), far_pass[i])

    def start_direct(i):
        start(both(has_far, jnp.logical_not(is_relayed(i))), far_direct[i])

    def relay(*items):
        for i in items:
            @pl.when(far_group[i] < partner_relayed)
            def _(i=i):
                far_pass[i].wait_recv()
                far_hop[i].start()

    start_pass(0)
    start(None, near_c0[0], n_mask, near_c0[1])
    start_pass(2, 4)
    start(None, near_r[0], near_r[1], near_c1[0], near_c1[1])
    for i in (0, 7, 4, 6, 2):
        start_direct(i)
    start(None, *direct_in)
    start(has_outer, *direct_out)
    start_pass(1, 5, 3)
    start(None, near_c0[2], near_r[2], near_c1[2], near_r[3], near_r[4])
    for i in (1, 5, 8, 3):
        start_direct(i)

    local_c = pltpu.make_async_copy(blocks, own_c, local_sem.at[0])
    own_rhs = ((0, 1, 0, 1), (0, 2, 1, 0), (1, 0, 0, 2), (1, 1, 1, 1))
    local_r = [pltpu.make_async_copy(rhs.at[rows[t], tx(k), 1], o_r.at[i], local_sem.at[1 + i])
               for i, (_, _, t, k) in enumerate(own_rhs)]
    local_n = pltpu.make_async_copy(counts, limits, local_sem.at[6])
    start(None, local_c, local_n, *local_r)

    def clear(*refs):
        for ref in refs:
            ref[...] = jnp.zeros(ref.shape, ref.dtype)

    @pl.when(jnp.logical_not(has_far))
    def _():
        clear(f_c0, f_c1, f_r, f_m, *[d.at[x, 1] for d in (d_c, d_r, d_m) for x in (0, 1)])

    @pl.when(jnp.logical_not(has_outer))
    def _():
        clear(g_c.at[1], g_r.at[1], g_m.at[1], d_c.at[1], d_r.at[1], d_m.at[1])

    wide_shape = (pairs, atoms * b)
    above, across = (lax.broadcasted_iota(jnp.int32, wide_shape, d) for d in (0, 1))
    spread = (above == atoms * (across // b) + across % b // orb).astype(F32)

    def widen(index, packed):
        for row in (0, 1):
            wide[index + row] = product(packed[:, pairs * row:pairs * row + pairs], spread)

    c_refs = (c_of0, c_of1, c_of2, c_of3)
    r_refs = (r_of0, r_of1, r_of2, r_of3)
    first_row = (0, 0, 1, 2)

    def put(w, s, k, j, value, mask):
        mask_row = wide[mask, pl.ds(3 * tx(k) + ty(j), 1), :]
        found = near_three(s)
        col = b * ((w + k - 1 - first_row[w]) * len(found) + s + j - 1 - found[0])
        masked = jnp.concatenate(
            [value[orb * i:orb * (i + 1)] * mask_row[:, b * i:b * (i + 1)] for i in range(atoms)],
            axis=0)
        high = masked.astype(BF16)
        rest = masked - high.astype(F32)
        c_refs[w][s, 0:b, col:col + b] = high
        c_refs[w][s, b:2 * b, col:col + b] = rest.astype(BF16)
        r_refs[w][s, :, col:col + b] = (rest * C_SCALE).astype(E4M3)

    def put_rhs(solve, u, s, value):
        at = b * (3 * u + s)
        basis[solve, 0, at:at + b, :] = value
        for part, piece in enumerate(split(value)):
            vec[solve, 0, at:at + b, b * part:b * part + b] = piece

    widen(0, own_m[...])
    local_c.wait()
    local_n.wait()
    for t in (0, 1):
        for k in range(3):
            for j in range(3):
                put(1 + t, 1, k, j, own_c[rows[t], tx(k), ty(j)], rows[t])
    for i, (solve, u, _, _) in enumerate(own_rhs):
        local_r[i].wait()
        put_rhs(solve, u, 1, o_r[i])

    arrived(None, *direct_in)
    widen(6, g_m[0])
    for k, slot in ((1, 1 - core), (2, core)):
        for j in range(3):
            put(0, 1, k, j, g_c[0, slot, ty(j)], 6 + core)
    put_rhs(0, 0, 1, g_r[0])

    n_mask.wait_recv()
    start(has_hop, f_mask)
    start(None, in_m[0])
    start(has_outer, out_m[0])
    relay(0)
    widen(2, n_m[...])

    def put_column(s, ref, t, k, j):
        put(1 + t, s, k, j, ref[rows[t], tx(k)], (2 if s == 2 else 4) + rows[t])

    near_c0[0].wait_recv()
    start(has_hop, far_c0[0])
    start(None, in_c[0][0])
    for k in range(3):
        put_column(2, n_c0, 0, k, 1)
    near_c0[1].wait_recv()
    start(has_hop, far_c0[1])
    start(has_outer, out_mid[0][0])
    for k in (0, 1):
        put_column(2, n_c0, 1, k, 1)
    relay(2, 4)
    arrived(None, near_r[0], near_r[1])
    start(None, in_r[0])
    put_rhs(0, 1, 2, n_r[rows[0], 1])
    put_rhs(0, 2, 2, n_r[rows[1], tx(0)])

    arrived(has_far, f_mask)
    start(has_far, in_m[1])
    start(both(has_far, has_outer), out_m[1])
    widen(4, f_m[...])
    arrived(has_far, far_direct[0], far_direct[7])
    start(has_far, in_r[1])
    put_rhs(0, 1, 0, f_r[rows[0], 1])
    put_rhs(0, 2, 0, f_r[rows[1], tx(0)])
    arrived(has_far, far_direct[4])
    start(has_far, in_c[1][1])
    arrived(has_far, far_direct[6], far_direct[2])
    start(both(has_far, has_outer), out_mid[1][1])
    for t, ks in ((0, (0, 1, 2)), (1, (0, 1))):
        for k in ks:
            put_column(0, f_c1, t, k, 2)
    arrived(has_far, far_c0[0], far_c0[1])
    start(has_far, in_c[1][0])
    start(both(has_far, has_outer), out_mid[1][0])
    for t, ks in ((0, (0, 1, 2)), (1, (0, 1))):
        for k in ks:
            put_column(0, f_c0, t, k, 1)

    arrived(has_outer, *direct_out)
    widen(8, g_m[1])
    for k, slot in ((1, core), (0, 1 - core)):
        for j in range(3):
            put(3, 1, k, j, g_c[1, slot, ty(j)], 9 - core)
    put_rhs(1, 2, 1, g_r[1])

    def put_corner(x, side, ways):
        s = 2 - 2 * side
        for way in ways:
            for k, slot in (((1, 1 - core), (2, core)), ((1, core), (0, 1 - core)))[x]:
                put(3 * x, s, k, 1 if way == 0 else 2 * side, d_c[x, side, way, slot],
                    10 + 2 * (2 * x + side) + (1 - core if x else core))

    def fold(value):
        return jnp.sum(value.reshape(-1, 8, b), axis=0)

    def column(value):
        return jnp.sum(value, axis=0, keepdims=True)

    def at_of(u, s):
        return slice(b * (3 * u + s), b * (3 * u + s) + b)

    members = [(u, s) for u in range(3) for s in range(3)]

    def apply_row(solve, turn, u, s, only=(0, 1, 2), low=True, scale=None):
        found = near_three(s)
        used = [k for k in found if k in only]
        if not used:
            return None
        strips = near_three(u)
        ref, first = c_refs[u + solve], strips[0] + solve - first_row[u + solve]
        height = slice(0, 2 * b if low else b)
        if len(used) == len(found):
            left = ref[s, height, b * len(found) * first:b * len(found) * (first + len(strips))]
        else:
            starts = [b * (len(found) * (first + i) + used[0] - found[0]) for i in range(len(strips))]
            left = jnp.concatenate(
                [ref[s, height, at:at + b * len(used)] for at in starts], axis=1)
        right = [vec[solve, turn, b * (3 * k + used[0]):b * (3 * k + used[0] + len(used)), :]
                 for k in strips]
        value = product(left, jnp.concatenate(right, axis=0))
        total = value[0:b, 0:b] + value[0:b, b:2 * b]
        if scale is not None:
            lanes = slice(b * len(found) * first, b * len(found) * (first + len(strips)))
            right = [coarse[solve, turn, b * (3 * k + found[0]):b * (3 * k + found[0] + len(found)), :]
                     for k in strips]
            return total + scale * product(
                r_refs[u + solve][s, :, lanes], jnp.concatenate(right, axis=0))
        return total + value[b:2 * b, 0:b] if low else total

    def before_near(solve, u, s):
        if solve == 0:
            return () if s == 2 else (0, 1, 2)
        return () if (u, s) == (2, 2) else (0, 1, 2) if s == 0 else (0, 1)

    def first_product(solve):
        for u, s in members:
            value = apply_row(solve, 0, u, s, before_near(solve, u, s))
            if value is not None:
                basis[solve, 1, at_of(u, s), :] = value

    def rest_of_first(solve, u, s):
        done = before_near(solve, u, s)
        value = apply_row(solve, 0, u, s, tuple(k for k in range(3) if k not in done))
        if not done:
            return value
        partial = basis[solve, 1, at_of(u, s), :]
        return partial if value is None else partial + value

    def solve_cluster(solve, between):
        gram = {}
        lengths = {}

        def power(j):
            square = gram[j - 1, j - 1]
            inverse = jnp.where(square > 0.0, lax.rsqrt(square), 0.0)
            lengths[j - 1] = square * inverse
            shrink = V_SCALE * inverse
            sums = [jnp.zeros((8, b), F32) for _ in range(j + 1)]
            for u, s in members:
                if j == 1:
                    value = rest_of_first(solve, u, s)
                else:
                    scale = lengths[j - 2] * (1.0 / (C_SCALE * V_SCALE))
                    value = apply_row(solve, (j - 1) % 2, u, s, low=False, scale=scale)
                basis[solve, j, at_of(u, s), :] = value
                if j < 2 * ITERS - 1:
                    coarse[solve, j % 2, at_of(u, s), :] = (value * shrink).astype(E5M2)
                for part, piece in enumerate(split(value)):
                    vec[solve, j % 2, at_of(u, s), b * part:b * part + b] = piece
                for i in range(j):
                    sums[i] = sums[i] + fold(value * basis[solve, i, at_of(u, s), :])
                sums[j] = sums[j] + fold(value * value)
            for i in range(j + 1):
                gram[i, j] = gram[j, i] = column(sums[i])
            between(j)

        def inner(left, other):
            result = None
            for i, a in enumerate(left):
                for k, c in enumerate(other):
                    term = (a * c) * gram[i, k]
                    result = term if result is None else result + term
            return result

        def norm_of(value):
            result = None
            for i, a in enumerate(value):
                for k in range(i, len(value)):
                    term = (a * value[k]) * gram[i, k] * (1.0 if i == k else 2.0)
                    result = term if result is None else result + term
            return jnp.maximum(result, 0.0)

        first_sums = jnp.zeros((8, b), F32)
        for u, s in members:
            value = basis[solve, 0, at_of(u, s), :]
            first_sums = first_sums + fold(value * value)
        gram[0, 0] = column(first_sums)
        count = limits[rows[solve]].astype(F32)
        atom_of = (lax.broadcasted_iota(jnp.int32, (atoms, b), 1) // orb
                   == lax.broadcasted_iota(jnp.int32, (atoms, b), 0)).astype(F32)
        limit = product(jnp.broadcast_to(count, (atoms, atoms)), atom_of)[0:1]

        power(1)
        norm = gram[0, 0]
        shadow = [jnp.ones_like(norm)]
        resid = y_first = shadow
        rho, floor = norm, 0.1 * norm
        tau = jnp.sqrt(norm)
        theta = eta = jnp.zeros_like(norm)
        u_first = along = image(y_first)
        direc, sol = [], []
        for n in range(1, ITERS + 1):
            active = (limit >= float(n)).astype(F32)
            if n > 1:
                power(2 * n - 1)
                rho_next = inner(shadow, resid)
                beta = guarded(rho_next, rho, floor)
                floor = 0.1 * jnp.sqrt(norm * size)
                rho = rho_next
                y_first = add(resid, beta, y_second)
                u_first = image(y_first)
                along = add(u_first, beta, add(u_second, beta, along))
            alpha = guarded(
                rho, inner(shadow, along), 0.1 * jnp.sqrt(norm * (norm_of(along) + 1e-06)))
            ratio = guarded(1.0, alpha, 0.1)
            y_second = add(y_first, -alpha, along)
            u_second = image(y_second)
            for part, (y, u_of) in enumerate(((y_first, u_first), (y_second, u_second))):
                resid = add(resid, -alpha, u_of)
                direc = add(y, theta * theta * eta * ratio, direc)
                if part == 1 and n == ITERS:
                    sums = jnp.zeros((8, b), F32)
                    for u, s in members:
                        value = apply_row(solve, (2 * n - 1) % 2, u, s, low=False)
                        value = value * resid[2 * n]
                        for i in range(2 * n):
                            value = value + basis[solve, i, at_of(u, s), :] * resid[i]
                        sums = sums + fold(value * value)
                    size = column(sums)
                else:
                    if part == 1:
                        power(2 * n)
                    size = norm_of(resid)
                theta = jnp.sqrt(size) / tau
                cosine = 1.0 / jnp.sqrt(1.0 + theta * theta)
                tau = tau * theta * cosine
                eta = cosine * cosine * alpha
                sol = add(sol, active * eta, direc)

        for u, s in members:
            value = basis[solve, 0, at_of(u, s), :] * sol[0]
            for i in range(1, 2 * ITERS):
                value = value + basis[solve, i, at_of(u, s), :] * sol[i]
            out[rows[solve], 3 * tx(u) + ty(s)] = value

    def between(j):
        if j == 1:
            relay(1, 5, 3)
            near_c0[2].wait_recv()
            start(has_hop, far_c0[2])
            start(has_outer, out_end[0][0])
            put_column(2, n_c0, 1, 2, 1)
        if j == 2:
            arrived(has_outer, out_m[0], *out_mid[0])
            arrived(both(has_far, has_outer), out_m[1], *out_mid[1])
            for side in (0, 1):
                widen(14 + 2 * side, d_m[1, side])
            near_r[2].wait_recv()
            start(has_outer, out_r[0])
        if j == 3:
            arrived(has_far, far_direct[1])
            start(both(has_far, has_outer), out_end[1][1])
            put_column(0, f_c1, 1, 2, 2)
        if j == 4:
            near_c1[2].wait_recv()
            start(has_outer, out_end[0][1])
            put_column(2, n_c1, 1, 2, 0)
            arrived(has_far, far_direct[5], far_direct[8])
            start(both(has_far, has_outer), out_r[1])
            put_rhs(1, 1, 0, f_r[rows[1], 1])
        if j == 5:
            arrived(has_far, far_c0[2], far_direct[3])
            start(both(has_far, has_outer), out_end[1][0])
            put_column(0, f_c0, 1, 2, 1)
            put_rhs(1, 0, 0, f_r[rows[0], tx(2)])

    arrived(has_far, in_m[1], in_r[1], *in_c[1])
    widen(12, d_m[0, 1])
    put_corner(0, 1, (0, 1))
    put_rhs(0, 0, 0, d_r[0, 1])
    arrived(None, in_m[0], in_r[0])
    widen(10, d_m[0, 0])
    put_rhs(0, 0, 2, d_r[0, 0])
    near_c1[0].wait_recv()
    start(None, in_c[0][1])
    first_product(0)
    near_c1[1].wait_recv()
    start(has_outer, out_mid[0][1])
    for t, ks in ((0, (0, 1, 2)), (1, (0, 1))):
        for k in ks:
            put_column(2, n_c1, t, k, 0)
    arrived(None, *in_c[0])
    put_corner(0, 0, (0, 1))
    solve_cluster(0, between)
    arrived(both(has_far, has_outer), out_r[1], *out_end[1])
    put_corner(1, 1, (0, 1))
    put_rhs(1, 2, 0, d_r[1, 1])
    first_product(1)
    arrived(has_outer, out_r[0], *out_end[0])
    put_corner(1, 0, (0, 1))
    put_rhs(1, 2, 2, d_r[1, 0])
    arrived(None, near_r[3], near_r[4])
    put_rhs(1, 1, 2, n_r[rows[1], 1])
    put_rhs(1, 0, 2, n_r[rows[0], tx(2)])
    solve_cluster(1, lambda j: None)

    sent(None, n_mask, *near_c0, *near_c1, *near_r, *direct_in, in_m[0], in_r[0], *in_c[0])
    sent(has_hop, f_mask, *far_c0)
    for i, copy in enumerate(far_direct):
        sent(both(has_far, jnp.logical_not(is_relayed(i))), copy)
    for i, copy in enumerate(far_pass):
        sent(is_relayed(i), copy)
        sent(far_group[i] < partner_relayed, far_hop[i])
    sent(has_outer, *direct_out)
    for side in (0, 1):
        if side:
            sent(has_far, in_m[1], in_r[1], *in_c[1])
        sent(has_outer if side == 0 else both(has_far, has_outer),
             out_m[side], out_r[side], *out_mid[side], *out_end[side])
    assert all(sum(1 for key in numbers if key[0] == kind) <= COPIES for kind in ("send", "recv"))


def shards(blocks, pair_mask, rhs_rows, counts):
    groups = blocks.shape[0]
    b = blocks.shape[-1]
    atoms = pair_mask.shape[-1]
    offsets = pair_mask.shape[2]
    blocks = blocks.reshape(groups, 3, 3, b, b)
    rhs = rhs_rows.reshape(groups, 3, 3, b, b)
    masks = pair_mask.transpose(0, 1, 3, 4, 2).reshape(groups, atoms, atoms, offsets)
    any_spec = pl.BlockSpec(memory_space=pl.ANY)
    vmem_spec = pl.BlockSpec(memory_space=pltpu.VMEM)

    def raw(*lead):
        return pltpu.VMEM(lead + (b, b), F32)

    def flags(*lead):
        return pltpu.VMEM(lead + (offsets, groups * atoms * atoms), F32)

    solved = pl.pallas_call(
        kernel,
        out_shape=pltpu.VMEM((groups, 9, b, b), F32),
        in_specs=[any_spec, any_spec, any_spec, any_spec],
        out_specs=vmem_spec,
        scratch_shapes=[
            raw(groups, 3, 3), raw(2, 2, 3), raw(groups, 3), raw(groups, 3), raw(groups, 3),
            raw(groups, 3), raw(2, 2, 2, 2), raw(9),
            raw(4), raw(2), raw(groups, 3), raw(groups, 3), raw(2, 2),
            pltpu.VMEM((groups, atoms, atoms, offsets), jnp.int32),
            flags(), flags(), flags(), flags(2), flags(2, 2),
            pltpu.VMEM(counts.shape, jnp.int32),
            pltpu.VMEM((18, offsets, atoms * b), F32),
            pltpu.VMEM((3, 2 * b, 6 * b), BF16),
            pltpu.VMEM((3, 2 * b, 9 * b), BF16),
            pltpu.VMEM((3, 2 * b, 9 * b), BF16),
            pltpu.VMEM((3, 2 * b, 6 * b), BF16),
            pltpu.VMEM((3, b, 6 * b), E4M3),
            pltpu.VMEM((3, b, 9 * b), E4M3),
            pltpu.VMEM((3, b, 9 * b), E4M3),
            pltpu.VMEM((3, b, 6 * b), E4M3),
            pltpu.VMEM((2, 2, 9 * b, 2 * b), BF16),
            pltpu.VMEM((2, 2, 9 * b, b), E5M2),
            pltpu.VMEM((2, 2 * ITERS, 9 * b, b), F32),
            pltpu.SemaphoreType.DMA((COPIES,)),
            pltpu.SemaphoreType.DMA((COPIES,)),
            pltpu.SemaphoreType.DMA((7,)),
        ],
        compiler_params=pltpu.CompilerParams(
            collective_id=0, has_side_effects=True, vmem_limit_bytes=60 * 1024 * 1024
        ),
    )(blocks, masks, rhs, counts)
    return solved.reshape(groups, 1, 9, b, b)


def solution(mesh):
    spec = P("gx", "gy", None, None, None)
    return jax.shard_map(
        shards,
        mesh=mesh,
        in_specs=(spec, spec, spec, P("gx", "gy", None)),
        out_specs=spec,
        check_vma=False,
    )
```
